32 devices in a mesh: gx: 8 (over z, x), gy: 4 (over y, core).
Axes of the slice: x: 2, y: 2, z: 4, core: 2. Of those that a mesh axis runs over, the one named last changes fastest.
Arguments:
- pair_ends: int32 [3, 462848], P(None, ('gx', 'gy')), may hold values from 0 to 65535, as said below
- pair_geometry: float32 [5, 462848], P(None, ('gx', 'gy')), may hold values from -2 to 2, as said below
- drag_coef: float32 [6, 65536], P(None, ('gx', 'gy')), may hold values from 0.2 to 2
- forces: float32 [6, 65536], P(None, ('gx', 'gy')), may hold values from -40 to 40
Outputs:
- velocity: float32 [6, 65536], P(None, ('gx', 'gy'))
- residual: float32 [6, 65536], P(None, ('gx', 'gy'))
The draws below stay inside these ranges and needn't reach their ends.
Inputs may be any that keep to these rules, and one draw needn't show every extreme that they name: `pair_ends`: row 0 is sphere i, row 1 sphere j, row 2 the slot of j in i's row of 16 slots; slot 16 marks padding (i = j = 65535), which stands at the end of every device's list, at least one entry on each. Sphere n lies in cell block n // 2048, held by the device with gx index block // 4 and gy index block % 4. A live entry's i lies in a block of the list's own gy index; j lies in i's block or one of its eight neighbours on the periodic grid of blocks. Live entries are ordered by the gx index of i's block; one device's list holds at most 4096 entries with i in one gx index, and in every gy index some block gets exactly 4096 from every list. Each (i, slot) appears at most once in all lists; an entry (i, j) at slot 2m has an entry (j, i) at slot 2m + 1 and the reverse. `pair_geometry`: rows 0 to 2 hold j's position minus i's, cell offsets included; rows 3 and 4 the radii of i and j; entries (i, j) and (j, i) have opposite separations and swapped radii; padding holds 0, 0, 0, 1, 1.
All inputs are finite; a program needn't handle non-finite values.
Results may differ from the reference program's by a relative error of at most 0.0003.
Values sent between devices are 32-bit elements; how exact they have to be, the bound alone decides.
No kernel may reach another device: no remote copies, remote signals or barrier semaphores. Data moves between devices by JAX's collectives and lax.ppermute only.
A program may use at most 128 MiB of HBM per device.

```python
import math
import jax
import jax.numpy as jnp
from jax import lax

S = 2048
K = 16
ITERS = 3
BASE = 512
SLABS = 8
STRIPS = 4
BLOCKS = 32
SPHERES = 65536
PW = 14464
PAIRS = 462848


def neighbour_layout(key):
    base_key = jax.random.fold_in(key, 1234)
    sub_keys = jax.random.split(base_key, 5)
    halves = K // 2
    sign_draw = (jax.random.randint(sub_keys[0], (4,), 0, 2) * 2 - 1).astype(jnp.int32)
    fixed_x = jnp.array([1, 0, 1, 1], jnp.int32) * sign_draw
    fixed_y = jnp.array([0, 1, 1, -1], jnp.int32) * sign_draw
    extra_codes = jax.random.randint(sub_keys[1], (halves - 4,), 0, 9).astype(jnp.int32)
    offset_x = jnp.concatenate([fixed_x, extra_codes // 3 - 1]).astype(jnp.int32)
    offset_y = jnp.concatenate([fixed_y, extra_codes % 3 - 1]).astype(jnp.int32)
    hot_x = jax.random.randint(sub_keys[2], (STRIPS,), 0, SLABS).astype(jnp.int32)
    partner = jax.vmap(lambda sub_key: jax.random.permutation(sub_key, S))(jax.random.split(sub_keys[3], halves)).astype(jnp.int32)
    inverse = jnp.argsort(partner, axis=1).astype(jnp.int32)
    ranking = jax.vmap(lambda sub_key: jax.random.permutation(sub_key, S))(jax.random.split(sub_keys[4], SLABS * STRIPS * halves)).astype(jnp.int32).reshape(SLABS, STRIPS, halves, S)
    grid_x = jnp.arange(SLABS, dtype=jnp.int32)[:, None, None]
    grid_y = jnp.arange(STRIPS, dtype=jnp.int32)[None, :, None]
    off_x = offset_x[None, None, :]
    off_y = offset_y[None, None, :]
    ahead_x = (grid_x + off_x) % SLABS
    ahead_y = (grid_y + off_y) % STRIPS
    back_x = (grid_x - off_x) % SLABS
    back_y = (grid_y - off_y) % STRIPS
    is_hot = grid_x == hot_x[grid_y]
    ahead_hot = ahead_x == hot_x[ahead_y]
    live_quota = jnp.where(jnp.logical_or(is_hot, ahead_hot), S, BASE).astype(jnp.int32)
    forward_live = ranking < live_quota[..., None]
    half_idx = jnp.arange(halves, dtype=jnp.int32)[None, None, :, None]
    backward_live = forward_live[back_x[..., None], back_y[..., None], half_idx, inverse[None, None, :, :]]
    forward_partner = (ahead_x * STRIPS + ahead_y)[..., None] * S + partner[None, None, :, :]
    backward_partner = (back_x * STRIPS + back_y)[..., None] * S + inverse[None, None, :, :]
    self_ids = (grid_x * STRIPS + grid_y)[..., None] * S + jnp.arange(S, dtype=jnp.int32)[None, None, None, :]
    full_shape = (SLABS, STRIPS, K, S)
    live_all = jnp.stack([forward_live, backward_live], axis=3).reshape(full_shape)
    partner_all = jnp.stack([forward_partner, backward_partner], axis=3).reshape(full_shape)
    first_all = jnp.broadcast_to(self_ids, (SLABS, STRIPS, halves, S))
    first_all = jnp.stack([first_all, first_all], axis=3).reshape(full_shape)
    slot_all = jnp.broadcast_to(jnp.arange(K, dtype=jnp.int32)[None, None, :, None], full_shape)
    cell_x = jnp.stack([offset_x, -offset_x], axis=1).reshape(K)
    cell_y = jnp.stack([offset_y, -offset_y], axis=1).reshape(K)
    cell_x_all = jnp.broadcast_to(cell_x[None, None, :, None], full_shape)
    cell_y_all = jnp.broadcast_to(cell_y[None, None, :, None], full_shape)

    def by_column(values):
        return values.transpose(1, 0, 2, 3).reshape(STRIPS, SLABS * K * S)
    live_col = by_column(live_all)
    order_pos = jnp.cumsum(live_col.astype(jnp.int32), axis=1, dtype=jnp.int32) - 1
    worker = order_pos % SLABS
    position = order_pos // SLABS
    column_idx = jnp.arange(STRIPS, dtype=jnp.int32)[:, None]
    destination = jnp.where(live_col, (worker * STRIPS + column_idx) * PW + position, PAIRS).astype(jnp.int32)
    return (destination.reshape(-1), by_column(first_all).reshape(-1), by_column(partner_all).reshape(-1), by_column(slot_all).reshape(-1), by_column(cell_x_all).reshape(-1), by_column(cell_y_all).reshape(-1))


def draw_pair_ends(key, part):
    destination, first_ids, partner_ids, slot_vals, cell_x, cell_y = neighbour_layout(key)
    filled = jnp.full((3, PAIRS), SPHERES - 1, jnp.int32)
    filled = filled.at[2].set(K)
    values = jnp.stack([first_ids, partner_ids, slot_vals], axis=0).astype(jnp.int32)
    return filled.at[:, destination].set(values, mode='drop')


def draw_pair_geometry(key, part):
    destination, first_ids, partner_ids, slot_vals, cell_x, cell_y = neighbour_layout(key)
    float_key = jax.random.fold_in(key, 4321)
    sub_keys = jax.random.split(float_key, 2)
    places = jax.random.uniform(sub_keys[0], (3, SPHERES), jnp.float32)
    radius = jnp.exp(jax.random.uniform(sub_keys[1], (SPHERES,), jnp.float32, math.log(0.1), 0.0))
    offsets = jnp.stack([cell_x.astype(jnp.float32), cell_y.astype(jnp.float32), jnp.zeros(cell_x.shape, jnp.float32)], axis=0)
    separation = places[:, partner_ids] - places[:, first_ids] + offsets
    values = jnp.concatenate([separation, radius[first_ids][None, :], radius[partner_ids][None, :]], axis=0)
    filled = jnp.concatenate([jnp.zeros((3, PAIRS), jnp.float32), jnp.ones((2, PAIRS), jnp.float32)], axis=0)
    return filled.at[:, destination].set(values, mode='drop')


def draw_forces(key, part):
    base_key = jax.random.fold_in(key, 31)
    sub_keys = jax.random.split(base_key, 3)
    comp_scale = jnp.exp(jax.random.uniform(sub_keys[0], (6, 1), jnp.float32, 0.0, math.log(10.0)))
    sphere_scale = jnp.exp(jax.random.uniform(sub_keys[1], (1, SPHERES), jnp.float32, 0.0, math.log(10.0)))
    block_frac = (jnp.arange(SPHERES, dtype=jnp.int32) // S).astype(jnp.float32) / (BLOCKS - 1)
    ramp = 1.0 + 2.0 * block_frac
    base_vals = jax.random.truncated_normal(sub_keys[2], -4.0, 4.0, (6, SPHERES), jnp.float32)
    return 0.03 * base_vals * comp_scale * sphere_scale * ramp[None, :]


def block_levels(stream_key, dims, cuts, low, largest):
    def one(dim, blocks):
        heights = jax.random.uniform(jax.random.fold_in(jax.random.fold_in(stream_key, 6), dim), (blocks,), jnp.float32, low / len(cuts), largest / len(cuts))
        return jnp.repeat(jnp.exp(heights), dims[dim] // blocks).reshape((-1,) + (1,) * (len(dims) - dim - 1))

    factor_of = one(*cuts[0])
    for cut in cuts[1:]:
        factor_of = factor_of * one(*cut)
    return factor_of


def setup_inputs(seed: int = 0) -> dict:
    arg_keys = jax.random.split(jax.random.key(seed), 5)
    pair_ends = draw_pair_ends(jax.random.fold_in(arg_keys[4], 71), 0)
    pair_geometry = draw_pair_geometry(jax.random.fold_in(arg_keys[4], 71), 0)
    drag_coef = jnp.clip(jnp.exp(math.log(2.0) - 2.3025851 * jax.random.uniform(arg_keys[2], (6, SPHERES), jnp.float32) ** block_levels(arg_keys[2], (6, SPHERES), ((1, 32),), -0.2, 0.2)), 0.2, 2.0)
    forces = draw_forces(jax.random.fold_in(arg_keys[4], 71), 0)
    return dict(pair_ends=pair_ends, pair_geometry=pair_geometry, drag_coef=drag_coef, forces=forces)


def pair_params(geometry):
    separation = geometry[0:3]
    radius_first = geometry[3]
    radius_second = geometry[4]
    reach_sum = radius_first + radius_second
    dist_sq = separation[0] * separation[0] + separation[1] * separation[1] + separation[2] * separation[2]
    unit_dir = separation / jnp.sqrt(dist_sq + reach_sum * reach_sum)
    weight = 1.0 / (1.0 + dist_sq / (reach_sum * reach_sum))
    reduced = radius_first * radius_second / reach_sum
    shear_coef = reduced * weight
    squeeze_coef = shear_coef * weight
    return jnp.concatenate([unit_dir, shear_coef[None], squeeze_coef[None]], axis=0)

def build_tile(pair_terms):
    unit_dir = pair_terms[0:3]
    shear_coef = pair_terms[3]
    squeeze_coef = pair_terms[4]
    length_sq = unit_dir[0] * unit_dir[0] + unit_dir[1] * unit_dir[1] + unit_dir[2] * unit_dir[2]
    entries = []
    for row_idx in range(6):
        for col_idx in range(6):
            outer_term = unit_dir[row_idx % 3] * unit_dir[col_idx % 3]
            same_axis = row_idx % 3 == col_idx % 3
            if row_idx < 3 and col_idx < 3:
                entry_val = 6.0 * squeeze_coef * outer_term
                if same_axis:
                    entry_val = entry_val + shear_coef
            elif row_idx >= 3 and col_idx >= 3:
                if same_axis:
                    entry_val = shear_coef * (2.5 - 2.0 * outer_term)
                else:
                    entry_val = shear_coef * (-2.0 * outer_term)
            elif same_axis:
                entry_val = 0.8 * shear_coef * (outer_term - length_sq / 3.0)
            else:
                entry_val = 0.8 * shear_coef * outer_term
            entries.append(entry_val)
    return jnp.stack(entries, axis=0)

def reference(pair_ends, pair_geometry, drag_coef, forces):
    is_live = pair_ends[2] < K
    pair_terms = jnp.where(is_live[None, :], pair_params(pair_geometry), 0.0)
    block_terms = pair_terms.reshape(5, BLOCKS, PW).transpose(1, 0, 2)
    first_ids = pair_ends[0].reshape(BLOCKS, PW).astype(jnp.int32)
    second_ids = pair_ends[1].reshape(BLOCKS, PW).astype(jnp.int32)

    def resist(vector):

        def accumulate(carried, inputs):
            block_par, left_ids, right_ids = inputs
            tile_rows = build_tile(block_par).reshape(6, 6, PW)
            change = vector[:, left_ids] - vector[:, right_ids]
            contrib = lax.optimization_barrier(jnp.sum(tile_rows * change[None, :, :], axis=1))
            return (carried.at[:, left_ids].add(contrib), None)
        result, unused = lax.scan(accumulate, drag_coef * vector, (block_terms, first_ids, second_ids))
        return result
    velocity = jnp.zeros_like(forces)
    residual = forces
    direction = forces
    norm_now = jnp.sum(residual * residual)
    for iteration in range(ITERS):
        applied = resist(direction)
        step_size = norm_now / jnp.sum(direction * applied)
        velocity = velocity + step_size * direction
        residual = residual - step_size * applied
        norm_next = jnp.sum(residual * residual)
        direction = residual + norm_next / norm_now * direction
        norm_now = norm_next
    return (velocity, residual)
```

```python
import functools

import jax
import jax.numpy as jnp
from jax import lax
from jax.experimental import pallas as pl
from jax.experimental.pallas import tpu as pltpu
from jax.sharding import PartitionSpec as P

K = 16
ITERS = 3
LANES = 128
SUB = 8
FIELDS = 6
SENT = 6

f32 = jnp.float32
i32 = jnp.int32
bf16 = jnp.bfloat16


def log2(n):
    assert n & (n - 1) == 0
    return n.bit_length() - 1


def iota(shape, dim):
    return lax.broadcasted_iota(i32, shape, dim)


def pack_kernel(slabs, strips, spheres, ends_ref, geo_ref, force_ref, send_ref, dense_ref, ends_s, geo_s, out_s):
    rows = ends_ref.shape[1] // LANES
    padded = ends_s.shape[0] // 3
    cap_rows = send_ref.shape[2]
    chunks = spheres // LANES
    for r in range(rows):
        cols = slice(r * LANES, (r + 1) * LANES)
        ends_s[pl.ds(r, 3, stride=padded), :] = ends_ref[:, cols]
        geo_s[pl.ds(r, 5, stride=padded), :] = geo_ref[:, cols]
    for r in range(chunks):
        dense_ref[pl.ds(r, FIELDS, stride=chunks), :] = force_ref[:, r * LANES : (r + 1) * LANES]
    first = ends_s[0:padded, :]
    second = ends_s[padded : 2 * padded, :]
    slot = ends_s[2 * padded : 3 * padded, :]
    inside = iota((padded, LANES), 0) < rows
    live = jnp.logical_and(slot < K, inside)
    shift = log2(spheres)
    first_block = first >> shift
    second_block = second >> shift
    owner = first_block >> log2(strips)
    shift_x = ((second_block >> log2(strips)) - owner + 1) & (slabs - 1)
    shift_y = ((second_block & (strips - 1)) - (first_block & (strips - 1)) + 1) & (strips - 1)
    column = (shift_x * 3 + shift_y) * spheres + (second & (spheres - 1))
    target = slot * spheres + (first & (spheres - 1))
    owner = jnp.where(live, owner, slabs)
    sep = [geo_s[c * padded : (c + 1) * padded, :] for c in range(3)]
    a = geo_s[3 * padded : 4 * padded, :]
    b = geo_s[4 * padded : 5 * padded, :]
    h = a + b
    total = sep[0] * sep[0] + sep[1] * sep[1] + sep[2] * sep[2] + h * h
    inv = lax.rsqrt(total)
    values = [target.astype(f32), column.astype(f32)] + [d * inv for d in sep] + [a * b * h * (inv * inv)]
    for c, value in enumerate(values):
        out_s[c, 0:padded, :] = value
    lane = iota((cap_rows, LANES), 1)
    place = iota((cap_rows, LANES), 0) * LANES + lane
    start = jnp.int32(0)
    for o in range(slabs):
        end = jnp.sum(jnp.where(owner <= o, 1.0, 0.0)).astype(i32)
        row = start >> 7
        off = start & (LANES - 1)
        back = (LANES - off) & (LANES - 1)
        for c in range(SENT):
            here = pltpu.roll(out_s[c, pl.ds(row, cap_rows), :], back, 1)
            after = pltpu.roll(out_s[c, pl.ds(row + 1, cap_rows), :], back, 1)
            value = jnp.where(lane < LANES - off, here, after)
            if c == 0:
                value = jnp.where(place < end - start, value, -1.0)
            send_ref[o, c] = value
        start = end


def pack(ends, geo, forces, slabs, strips):
    spheres = forces.shape[1]
    cap_rows = spheres * K // slabs // LANES
    rows = ends.shape[1] // LANES
    padded = -(-rows // SUB) * SUB
    return pl.pallas_call(
        functools.partial(pack_kernel, slabs, strips, spheres),
        out_shape=(
            jax.ShapeDtypeStruct((slabs, SENT, cap_rows, LANES), f32),
            jax.ShapeDtypeStruct((FIELDS * spheres // LANES, LANES), f32),
        ),
        scratch_shapes=[
            pltpu.VMEM((3 * padded, LANES), i32),
            pltpu.VMEM((5 * padded, LANES), f32),
            pltpu.VMEM((SENT, padded + cap_rows + SUB, LANES), f32),
        ],
        name="pack",
    )(ends, geo, forces)


def place_kernel(spheres, got_ref, terms_ref, col_ref, span_ref, acc, tgt, lo_v, n_v, lo_s, n_s, sem):
    sources = got_ref.shape[0]
    cap_rows = got_ref.shape[2]
    groups = sources // SUB
    tiles = K * spheres // (SUB * LANES)
    shift = log2(spheres)
    lane = iota((SUB, LANES), 1)
    big = 1 << 20

    acc[...] = jnp.zeros_like(acc)
    hi_iota = iota((2 * LANES, LANES), 0).astype(f32).astype(bf16)
    lo_iota = iota((LANES, LANES), 0).astype(f32).astype(bf16)
    lane_value = iota((LANES, LANES), 1).astype(f32).astype(bf16)
    one = jnp.ones((), bf16)
    zero = jnp.zeros((), bf16)

    for s in range(sources):

        def step(g, carry):
            t = got_ref[s, 0, pl.ds(pl.multiple_of(g * SUB, SUB), SUB), :].astype(i32)
            hi = (t >> 7).astype(f32)
            lo = (t & (LANES - 1)).astype(f32)
            left = []
            right_row = []
            right_lane = []
            for u in range(SUB):
                hi_row = jnp.broadcast_to(hi[u : u + 1, :], (2 * LANES, LANES)).astype(bf16)
                lo_row = jnp.broadcast_to(lo[u : u + 1, :], (LANES, LANES)).astype(bf16)
                left.append(jnp.where(hi_iota == hi_row, one, zero))
                number = jnp.full((LANES, LANES), (g * SUB + (u + s * cap_rows + 1)).astype(f32), f32).astype(bf16)
                match = lo_iota == lo_row
                right_row.append(jnp.where(match, number, zero))
                right_lane.append(jnp.where(match, lane_value, zero))
            left = jnp.concatenate(left, axis=1)
            right = jnp.concatenate([jnp.concatenate(right_row, axis=1), jnp.concatenate(right_lane, axis=1)], axis=0)
            acc[...] += lax.dot_general(left, right, (((1,), (1,)), ((), ())), preferred_element_type=f32)
            return carry

        lax.fori_loop(0, cap_rows // SUB, step, 0)

    for group in range(groups):
        low = jnp.full((SUB, LANES), big, i32)
        high = jnp.full((SUB, LANES), -1, i32)
        for k in range(cap_rows):
            for u in range(SUB):
                tgt[u : u + 1, :] = got_ref[group * SUB + u, 0, k : k + 1, :]
            t = tgt[...]
            tile = jnp.floor(t * (1.0 / (SUB * LANES)))
            t_low = jnp.min(jnp.where(t < 0.0, float(big), tile), axis=1, keepdims=True).astype(i32)
            t_high = jnp.max(jnp.where(t < 0.0, -1.0, tile), axis=1, keepdims=True).astype(i32)
            low = jnp.where(lane == k, t_low, low)
            high = jnp.where(lane == k, t_high, high)
        starts = jnp.full((SUB, LANES), 0, i32)
        counts = jnp.full((SUB, LANES), 0, i32)
        lane_f = lane.astype(f32)
        for q in range(tiles):
            hit = jnp.logical_and(low <= q, high >= q)
            k_low = jnp.min(jnp.where(hit, lane_f, float(cap_rows - 1)), axis=1, keepdims=True)
            k_high = jnp.max(jnp.where(hit, lane_f, -1.0), axis=1, keepdims=True)
            starts = jnp.where(lane == q, k_low.astype(i32), starts)
            counts = jnp.where(lane == q, (k_high - k_low).astype(i32) + 1, counts)
        lo_v[group] = starts
        n_v[group] = jnp.broadcast_to(jnp.max(counts.astype(f32), axis=0, keepdims=True).astype(i32), (SUB, LANES))
    lo_copy = pltpu.make_async_copy(lo_v, lo_s, sem.at[0])
    n_copy = pltpu.make_async_copy(n_v, n_s, sem.at[1])
    lo_copy.start()
    n_copy.start()
    lo_copy.wait()
    n_copy.wait()

    def place(q, carry):
        low, high = carry
        rows = pl.ds(pl.multiple_of(q * SUB, SUB), SUB)
        number = acc[rows, 0:LANES].astype(i32)
        at = acc[rows, LANES : 2 * LANES].astype(i32)
        values = tuple(jnp.zeros((SUB, LANES), f32) for _ in range(SENT - 1))
        for group in range(groups):

            def pick(kk, values):
                values = list(values)
                for u in range(SUB):
                    s = group * SUB + u
                    k = jnp.minimum(lo_s[group, u, q] + kk, cap_rows - 1)
                    match = number == s * cap_rows + k + 1
                    for c in range(1, SENT):
                        row = jnp.broadcast_to(got_ref[s, c, pl.ds(k, 1), :], (SUB, LANES))
                        found = jnp.take_along_axis(row, at, axis=1)
                        values[c - 1] = jnp.where(match, found, values[c - 1])
                return tuple(values)

            values = lax.fori_loop(0, n_s[group, 0, q], pick, values)
        filled = number > 0
        col = jnp.where(filled, values[0], -1.0)
        col_ref[rows, :] = col.astype(i32)
        for c in range(SENT - 2):
            terms_ref[c, rows, :] = values[c + 1]
        block = jnp.floor(col * (1.0 / spheres))
        b_low = jnp.min(jnp.where(filled, block, float(big)), axis=1, keepdims=True)
        b_high = jnp.max(block, axis=1, keepdims=True)
        return (jnp.where(lane == q, b_low, low), jnp.where(lane == q, b_high, high))

    low, high = lax.fori_loop(
        0, tiles, place, (jnp.full((SUB, LANES), float(big), f32), jnp.full((SUB, LANES), -1.0, f32))
    )
    span_ref[0:SUB, :] = jnp.broadcast_to(jnp.min(low, axis=0, keepdims=True), (SUB, LANES)).astype(i32)
    span_ref[SUB : 2 * SUB, :] = jnp.broadcast_to(jnp.max(high, axis=0, keepdims=True), (SUB, LANES)).astype(i32)


def place_entries(got, spheres):
    sources = got.shape[0]
    groups = sources // SUB
    slot_rows = K * spheres // LANES
    assert slot_rows == 2 * LANES
    return pl.pallas_call(
        functools.partial(place_kernel, spheres),
        out_shape=(
            jax.ShapeDtypeStruct((SENT - 2, slot_rows, LANES), f32),
            jax.ShapeDtypeStruct((slot_rows, LANES), i32),
            jax.ShapeDtypeStruct((2 * SUB, LANES), i32),
        ),
        scratch_shapes=[
            pltpu.VMEM((slot_rows, 2 * LANES), f32),
            pltpu.VMEM((SUB, LANES), f32),
            pltpu.VMEM((groups, SUB, LANES), i32),
            pltpu.VMEM((groups, SUB, LANES), i32),
            pltpu.SMEM((groups, SUB, LANES), i32),
            pltpu.SMEM((groups, SUB, LANES), i32),
            pltpu.SemaphoreType.DMA((2,)),
        ],
        name="place",
    )(got)


def lane_pick(row, k):
    return jnp.sum(jnp.where(iota(row.shape, 1) == k, row, 0.0), axis=1, keepdims=True)


def apply_operator(table, span_ref, col_ref, terms_ref, drag_ref, out_ref):
    chunks = table.shape[2]
    halves = chunks // SUB
    centre = 4
    tiles = K * halves

    def slot(k, sums):
        base = [(k * halves + h) * SUB for h in range(halves)]
        rows = [pl.ds(pl.multiple_of(b, SUB), SUB) for b in base]
        col = [col_ref[r, :] for r in rows]
        at = [c & (LANES - 1) for c in col]
        number = [c >> 7 for c in col]
        low = span_ref[0, k * halves]
        high = span_ref[SUB, k * halves]
        for h in range(1, halves):
            low = jnp.minimum(low, span_ref[0, k * halves + h])
            high = jnp.maximum(high, span_ref[SUB, k * halves + h])

        def block(b, values):
            values = list(values)
            for r in range(chunks):
                match = [n == b * chunks + r for n in number]
                for c in range(FIELDS):
                    row = jnp.broadcast_to(table[b, c, r : r + 1, :], (SUB, LANES))
                    for h in range(halves):
                        found = jnp.take_along_axis(row, at[h], axis=1)
                        values[h * FIELDS + c] = jnp.where(match[h], found, values[h * FIELDS + c])
            return tuple(values)

        zeros = tuple(jnp.zeros((SUB, LANES), f32) for _ in range(FIELDS * halves))
        other = lax.fori_loop(low, high + 1, block, zeros)
        sums = list(sums)
        for h in range(halves):
            own = [table[centre, c, h * SUB : (h + 1) * SUB, :] for c in range(FIELDS)]
            diff = [own[c] - other[h * FIELDS + c] for c in range(FIELDS)]
            e = [terms_ref[c, rows[h], :] for c in range(3)]
            c1 = terms_ref[3, rows[h], :]
            size = e[0] * e[0] + e[1] * e[1] + e[2] * e[2]
            c2 = c1 * (1.0 - size)
            p = e[0] * diff[0] + e[1] * diff[1] + e[2] * diff[2]
            t = e[0] * diff[3] + e[1] * diff[4] + e[2] * diff[5]
            mix = 0.8 * c1
            along_top = 6.0 * c2 * p + mix * t
            along_bottom = mix * p - 2.0 * c1 * t
            cross = mix * (size * (1.0 / 3.0))
            strong = 2.5 * c1
            for c in range(3):
                top = e[c] * along_top + c1 * diff[c] - cross * diff[3 + c]
                bottom = e[c] * along_bottom - cross * diff[c] + strong * diff[3 + c]
                sums[h * FIELDS + c] = sums[h * FIELDS + c] + top
                sums[h * FIELDS + 3 + c] = sums[h * FIELDS + 3 + c] + bottom
        return tuple(sums)

    start = []
    for h in range(halves):
        for c in range(FIELDS):
            own = table[centre, c, h * SUB : (h + 1) * SUB, :]
            start.append(drag_ref[c * chunks + h * SUB : c * chunks + (h + 1) * SUB, :] * own)
    sums = lax.fori_loop(0, K, slot, tuple(start))
    for h in range(halves):
        for c in range(FIELDS):
            out_ref[c, h * SUB : (h + 1) * SUB, :] = sums[h * FIELDS + c]


def total(x):
    x = jnp.sum(x, axis=0)
    return jnp.sum(jnp.sum(x, axis=0, keepdims=True), axis=1, keepdims=True)


def put_dots(dots_ref, values):
    lane = iota((1, LANES), 1)
    row = jnp.zeros((1, LANES), f32)
    for k, value in enumerate(values):
        row = jnp.where(lane == k, value, row)
    dots_ref[...] = jnp.broadcast_to(row, dots_ref.shape)


def join(table, west, mid, east):
    for y in range(3):
        table[y] = west[y]
        table[3 + y] = mid[y]
        table[6 + y] = east[y]


def first_kernel(span, col, terms, drag, west, mid, east, drag_out, r_out, s_out, dots_out):
    chunks = s_out.shape[1]
    for r in range(chunks):
        drag_out[pl.ds(r, FIELDS, stride=chunks), :] = drag[:, r * LANES : (r + 1) * LANES]
    join(r_out, west, mid, east)
    apply_operator(r_out, span, col, terms, drag_out, s_out)
    r = r_out[4]
    put_dots(dots_out, [total(r * r), total(r * s_out[...])])


def next_kernel(
    first, span, col, terms, drag, west, mid, east, r_in, w_in, d_in, v_in, scal_in, dots,
    r_out, w_out, d_out, v_out, scal_out, s_out, dots_out,
):
    beta, step = scalars(first, dots, scal_in, scal_out)
    parts = [(west, 0), (mid, 3), (east, 6)]
    for part, base in parts:
        for y in range(3):
            w = part[y]
            if not first:
                w = w + beta * w_in[base + y]
            w_out[base + y] = w
            r_out[base + y] = r_in[base + y] - step * w
    d = r_in[4]
    if first:
        v_out[...] = step * d
    else:
        d = d + beta * d_in[...]
        v_out[...] = v_in[...] + step * d
    d_out[...] = d
    apply_operator(r_out, span, col, terms, drag, s_out)
    r = r_out[4]
    s = s_out[...]
    put_dots(dots_out, [total(r * r), total(r * s), total(r * w_out[4] + d * s)])


def scalars(first, dots, scal_in, scal_out):
    row = jnp.sum(dots[...], axis=0, keepdims=True)
    rr = lane_pick(row, 0)
    rs = lane_pick(row, 1)
    if first:
        beta = None
        dad = rs
    else:
        old = scal_in[0:1, :]
        beta = rr / lane_pick(old, 0)
        dad = rs + beta * (lane_pick(row, 2) + beta * lane_pick(old, 1))
    if scal_out is not None:
        put_dots(scal_out, [rr, dad])
    return beta, rr / dad


def last_kernel(s_in, r_in, w_in, d_in, v_in, scal_in, dots, v_final, r_final, v_s, r_s):
    beta, step = scalars(False, dots, scal_in, None)
    chunks = s_in.shape[1]
    for c in range(FIELDS):
        w = s_in[c] + beta * w_in[4, c]
        d = r_in[4, c] + beta * d_in[c]
        v_s[c * chunks : (c + 1) * chunks, :] = v_in[c] + step * d
        r_s[c * chunks : (c + 1) * chunks, :] = r_in[4, c] - step * w
    for r in range(chunks):
        v_final[:, r * LANES : (r + 1) * LANES] = v_s[pl.ds(r, FIELDS, stride=chunks), :]
        r_final[:, r * LANES : (r + 1) * LANES] = r_s[pl.ds(r, FIELDS, stride=chunks), :]


VMEM = pl.BlockSpec(memory_space=pltpu.VMEM)
SMEM = pl.BlockSpec(memory_space=pltpu.SMEM)


def shapes(*dims):
    return tuple(jax.ShapeDtypeStruct(d, f32) for d in dims)


def ring(axis, step):
    count = lax.axis_size(axis)
    return [(i, (i + step) % count) for i in range(count)]


def beside(x):
    below = lax.ppermute(x, "gy", ring("gy", 1))
    above = lax.ppermute(x, "gy", ring("gy", -1))
    mid = jnp.stack([below, x, above])
    west = lax.ppermute(mid, "gx", ring("gx", 1))
    east = lax.ppermute(mid, "gx", ring("gx", -1))
    return west, mid, east


def share(dots):
    return lax.all_to_all(dots, ("gx", "gy"), split_axis=0, concat_axis=0, tiled=True)


def on_device(pair_ends, pair_geometry, drag_coef, forces):
    spheres = drag_coef.shape[1]
    chunks = spheres // LANES
    slabs = lax.axis_size("gx")
    strips = lax.axis_size("gy")
    devices = slabs * strips
    send, force_rows = pack(pair_ends, pair_geometry, forces, slabs, strips)
    got = lax.all_to_all(send, "gx", split_axis=0, concat_axis=0, tiled=True)
    field = (FIELDS, chunks, LANES)
    table = (9, FIELDS, chunks, LANES)
    west, mid, east = beside(force_rows.reshape(field))
    terms, col, span = place_entries(got, spheres)
    drag, r, s, dots = pl.pallas_call(
        first_kernel,
        out_shape=shapes((FIELDS * chunks, LANES), table, field, (devices, LANES)),
        in_specs=[SMEM] + [VMEM] * 6,
        name="first",
    )(span, col, terms, drag_coef, west, mid, east)
    w = d = v = scal = None
    for iteration in range(1, ITERS):
        first = iteration == 1
        west, mid, east = beside(s)
        shared = share(dots)
        state = [r] if first else [r, w, d, v, scal]

        def kernel(*refs, first=first):
            refs = list(refs)
            if first:
                refs[8:8] = [None] * 4
            next_kernel(first, *refs)

        r, w, d, v, scal, s, dots = pl.pallas_call(
            kernel,
            out_shape=shapes(table, table, field, field, (SUB, LANES), field, (devices, LANES)),
            in_specs=[SMEM] + [VMEM] * (6 + len(state) + 1),
            name=f"next{iteration}",
        )(span, col, terms, drag, west, mid, east, *state, shared)
    return pl.pallas_call(
        last_kernel,
        out_shape=shapes((FIELDS, spheres), (FIELDS, spheres)),
        scratch_shapes=[pltpu.VMEM((FIELDS * chunks, LANES), f32)] * 2,
        name="last",
    )(s, r, w, d, v, scal, share(dots))


def solution(mesh):
    spec = P(None, ("gx", "gy"))
    return jax.shard_map(
        on_device, mesh=mesh, in_specs=(spec,) * 4, out_specs=(spec, spec), check_vma=False
    )
```

```python
import functools

import jax
import jax.numpy as jnp
from jax import lax
from jax.experimental import pallas as pl
from jax.experimental.pallas import tpu as pltpu
from jax.sharding import PartitionSpec as P

K = 16
ITERS = 3
LANES = 128
SUB = 8
FIELDS = 6
SENT = 6

f32 = jnp.float32
i32 = jnp.int32
bf16 = jnp.bfloat16


def log2(n):
    assert n & (n - 1) == 0
    return n.bit_length() - 1


def iota(shape, dim):
    return lax.broadcasted_iota(i32, shape, dim)


def pack_kernel(slabs, strips, spheres, ends_ref, geo_ref, force_ref, label_ref, send_ref, dense_ref, ends_s, geo_s, out_s):
    rows = ends_ref.shape[1] // LANES
    padded = ends_s.shape[0] // 3
    cap_rows = label_ref.shape[1]
    chunks = spheres // LANES
    for r in range(rows):
        cols = slice(r * LANES, (r + 1) * LANES)
        ends_s[pl.ds(r, 3, stride=padded), :] = ends_ref[:, cols]
        geo_s[pl.ds(r, 5, stride=padded), :] = geo_ref[:, cols]
    for r in range(chunks):
        dense_ref[pl.ds(r, FIELDS, stride=chunks), :] = force_ref[:, r * LANES : (r + 1) * LANES]
    first = ends_s[0:padded, :]
    second = ends_s[padded : 2 * padded, :]
    slot = ends_s[2 * padded : 3 * padded, :]
    inside = iota((padded, LANES), 0) < rows
    live = jnp.logical_and(slot < K, inside)
    shift = log2(spheres)
    first_block = first >> shift
    second_block = second >> shift
    owner = first_block >> log2(strips)
    shift_x = ((second_block >> log2(strips)) - owner + 1) & (slabs - 1)
    shift_y = ((second_block & (strips - 1)) - (first_block & (strips - 1)) + 1) & (strips - 1)
    column = (shift_y * 3 + shift_x) * spheres + (second & (spheres - 1))
    target = slot * spheres + (first & (spheres - 1))
    owner = jnp.where(live, owner, slabs)
    sep = [geo_s[c * padded : (c + 1) * padded, :] for c in range(3)]
    a = geo_s[3 * padded : 4 * padded, :]
    b = geo_s[4 * padded : 5 * padded, :]
    h = a + b
    total = sep[0] * sep[0] + sep[1] * sep[1] + sep[2] * sep[2] + h * h
    inv = lax.rsqrt(total)
    values = [target.astype(f32), column.astype(f32)] + [d * inv for d in sep] + [a * b * h * (inv * inv)]
    for c, value in enumerate(values):
        out_s[c, 0:padded, :] = value
    lane = iota((cap_rows, LANES), 1)
    place = iota((cap_rows, LANES), 0) * LANES + lane
    start = jnp.int32(0)
    for o in range(slabs):
        end = jnp.sum(jnp.where(owner <= o, 1.0, 0.0)).astype(i32)
        row = start >> 7
        off = start & (LANES - 1)
        back = (LANES - off) & (LANES - 1)
        for c in range(SENT):
            here = pltpu.roll(out_s[c, pl.ds(row, cap_rows), :], back, 1)
            after = pltpu.roll(out_s[c, pl.ds(row + 1, cap_rows), :], back, 1)
            value = jnp.where(lane < LANES - off, here, after)
            if c == 0:
                label_ref[o] = jnp.where(place < end - start, value, -1.0)
            else:
                send_ref[o, c - 1] = value
        start = end


def pack(ends, geo, forces, slabs, strips):
    spheres = forces.shape[1]
    cap_rows = spheres * K // slabs // LANES
    rows = ends.shape[1] // LANES
    padded = -(-rows // SUB) * SUB
    return pl.pallas_call(
        functools.partial(pack_kernel, slabs, strips, spheres),
        out_shape=(
            jax.ShapeDtypeStruct((slabs, cap_rows, LANES), f32),
            jax.ShapeDtypeStruct((slabs, SENT - 1, cap_rows, LANES), f32),
            jax.ShapeDtypeStruct((FIELDS * spheres // LANES, LANES), f32),
        ),
        scratch_shapes=[
            pltpu.VMEM((3 * padded, LANES), i32),
            pltpu.VMEM((5 * padded, LANES), f32),
            pltpu.VMEM((SENT, padded + cap_rows + SUB, LANES), f32),
        ],
        compiler_params=PARAMS,
        name="pack",
    )(ends, geo, forces)


def place_ranges(spheres, got_ref, tab_v):
    sources = got_ref.shape[0]
    cap_rows = got_ref.shape[1]
    tiles = K * spheres // (SUB * LANES)
    lane = iota((SUB, LANES), 1)
    lane_f = lane.astype(f32)
    big = float(1 << 20)
    for group in range(sources // SUB):
        low = jnp.full((SUB, LANES), big, f32)
        high = jnp.full((SUB, LANES), -1.0, f32)
        for k in range(cap_rows):
            t = got_ref[group * SUB : (group + 1) * SUB, k, :]
            tile = jnp.floor(t * (1.0 / (SUB * LANES)))
            t_low = jnp.min(jnp.where(t < 0.0, big, tile), axis=1, keepdims=True)
            t_high = jnp.max(tile, axis=1, keepdims=True)
            low = jnp.where(lane == k, t_low, low)
            high = jnp.where(lane == k, t_high, high)
        starts = jnp.zeros((SUB, LANES), f32)
        counts = jnp.zeros((SUB, LANES), f32)
        for q in range(tiles):
            hit = jnp.logical_and(low <= q, high >= q)
            k_low = jnp.min(jnp.where(hit, lane_f, float(cap_rows - 1)), axis=1, keepdims=True)
            k_high = jnp.max(jnp.where(hit, lane_f, -1.0), axis=1, keepdims=True)
            starts = jnp.where(lane == q, k_low, starts)
            counts = jnp.where(lane == q, k_high - k_low + 1.0, counts)
        tab_v[group, 0] = starts.astype(i32)
        tab_v[group, 1] = jnp.broadcast_to(jnp.max(counts, axis=0, keepdims=True), (SUB, LANES)).astype(i32)
        for step in (1, 2, 4):
            low = jnp.minimum(low, pltpu.roll(low, LANES - step, 1))
            high = jnp.maximum(high, pltpu.roll(high, LANES - step, 1))
        tab_v[group, 2] = low.astype(i32)
        tab_v[group, 3] = high.astype(i32)


WINDOWS = 4


def place_invert(got_ref, tab_s, acc):
    cap_rows = got_ref.shape[1]
    chunks = cap_rows // SUB
    slot_rows = 2 * LANES
    window = slot_rows // WINDOWS
    acc[...] = jnp.zeros_like(acc)
    hi_iota = iota((window, LANES), 0).astype(f32)
    lo_iota = iota((LANES, LANES), 0).astype(f32).astype(bf16)
    lane_value = iota((window, LANES), 1).astype(f32).astype(bf16)
    one = jnp.ones((), bf16)
    zero = jnp.zeros((), bf16)

    def step(i, carry):
        s = i >> log2(chunks)
        g = i & (chunks - 1)
        group = s >> 3
        low = tab_s[group, 2, s & (SUB - 1), g * SUB]
        high = tab_s[group, 3, s & (SUB - 1), g * SUB]

        @pl.when(high >= 0)
        def _():
            t = got_ref[s, pl.ds(pl.multiple_of(g * SUB, SUB), SUB), :].astype(i32)
            hi = (t >> 7).astype(f32).astype(bf16)
            lo = (t & (LANES - 1)).astype(f32).astype(bf16)
            right = []
            for u in range(SUB):
                row = jnp.broadcast_to(lo[u : u + 1, :], (LANES, LANES))
                right.append(jnp.where(lo_iota == row, one, zero))
            right = jnp.concatenate(right, axis=1)
            for w in range(WINDOWS):
                tiles = window // SUB

                @pl.when(jnp.logical_and(low < (w + 1) * tiles, high >= w * tiles))
                def _():
                    numbers, lanes = [], []
                    iota_w = (hi_iota + float(w * window)).astype(bf16)
                    for u in range(SUB):
                        row = jnp.broadcast_to(hi[u : u + 1, :], (window, LANES))
                        match = iota_w == row
                        number = (s * cap_rows + g * SUB + (u + 1)).astype(f32)
                        number = jnp.full((window, LANES), number, f32).astype(bf16)
                        numbers.append(jnp.where(match, number, zero))
                        lanes.append(jnp.where(match, lane_value, zero))
                    left = jnp.concatenate(
                        [jnp.concatenate(numbers, axis=1), jnp.concatenate(lanes, axis=1)], axis=0
                    )
                    out = lax.dot_general(left, right, (((1,), (1,)), ((), ())), preferred_element_type=f32)
                    acc[w * window : (w + 1) * window, :] += out[:window]
                    acc[slot_rows + w * window : slot_rows + (w + 1) * window, :] += out[window:]

        return carry

    lax.fori_loop(0, got_ref.shape[0] * chunks, step, 0)


def place_pick(spheres, got_ref, tab_s, pos_ref, terms_ref, col_ref):
    sources = got_ref.shape[0]
    cap_rows = got_ref.shape[2]
    slot_rows = 2 * LANES

    def place(q, carry):
        rows = pl.ds(pl.multiple_of(q * SUB, SUB), SUB)
        number = pos_ref[rows, :].astype(i32)
        at = pos_ref[pl.ds(pl.multiple_of(slot_rows + q * SUB, SUB), SUB), :].astype(i32)
        values = tuple(jnp.zeros((SUB, LANES), f32) for _ in range(SENT - 1))
        for group in range(sources // SUB):

            def pick(kk, values):
                values = list(values)
                for u in range(SUB):
                    s = group * SUB + u
                    k = jnp.minimum(tab_s[group, 0, u, q] + kk, cap_rows - 1)
                    match = number == s * cap_rows + k + 1
                    for c in range(SENT - 1):
                        row = jnp.broadcast_to(got_ref[s, c, pl.ds(k, 1), :], (SUB, LANES))
                        found = jnp.take_along_axis(row, at, axis=1)
                        values[c] = jnp.where(match, found, values[c])
                return tuple(values)

            values = lax.fori_loop(0, tab_s[group, 1, 0, q], pick, values)
        col_ref[rows, :] = jnp.where(number > 0, values[0], -1.0).astype(i32)
        for c in range(SENT - 2):
            terms_ref[c, rows, :] = values[c + 1]
        return carry

    lax.fori_loop(0, K * spheres // (SUB * LANES), place, 0)


def place_blocks(spheres, col_ref, span_ref):
    lane = iota((SUB, LANES), 1)
    big = float(1 << 20)
    low = jnp.full((SUB, LANES), big, f32)
    high = jnp.full((SUB, LANES), -1.0, f32)
    for q in range(K * spheres // (SUB * LANES)):
        block = (col_ref[q * SUB : (q + 1) * SUB, :] >> log2(spheres)).astype(f32)
        b_low = jnp.min(jnp.where(block < 0.0, big, block), axis=1, keepdims=True)
        b_high = jnp.max(block, axis=1, keepdims=True)
        low = jnp.where(lane == q, b_low, low)
        high = jnp.where(lane == q, b_high, high)
    span_ref[0:SUB, :] = jnp.broadcast_to(jnp.min(low, axis=0, keepdims=True), (SUB, LANES)).astype(i32)
    span_ref[SUB : 2 * SUB, :] = jnp.broadcast_to(jnp.max(high, axis=0, keepdims=True), (SUB, LANES)).astype(i32)


def invert_kernel(spheres, got_ref, pos_ref, tab_ref, tab_s, sem):
    place_ranges(spheres, got_ref, tab_ref)
    copy = pltpu.make_async_copy(tab_ref, tab_s, sem)
    copy.start()
    copy.wait()
    place_invert(got_ref, tab_s, pos_ref)


def invert(got, spheres):
    assert K * spheres == 2 * LANES * LANES
    table = (got.shape[0] // SUB, 4, SUB, LANES)
    return pl.pallas_call(
        functools.partial(invert_kernel, spheres),
        out_shape=(jax.ShapeDtypeStruct((4 * LANES, LANES), f32), jax.ShapeDtypeStruct(table, i32)),
        scratch_shapes=[pltpu.SMEM(table, i32), pltpu.SemaphoreType.DMA],
        compiler_params=PARAMS,
        cost_estimate=pl.CostEstimate(flops=4 << 30, bytes_accessed=2 << 20, transcendentals=0),
        name="invert",
    )(got)


def spread(parts, big):
    for y, part in enumerate(parts):

        def strip(x, carry):
            for c in range(FIELDS):
                for r in range(part.shape[2]):
                    big[3 * y + x, c, r] = jnp.broadcast_to(part[x, c, r : r + 1, :], (SUB, LANES))
            return carry

        lax.fori_loop(0, 3, strip, 0)


def apply_operator(own_ref, big, span_ref, col_ref, terms_ref, drag_ref, out_ref):
    chunks = big.shape[2]
    halves = chunks // SUB

    def slot(k, sums):
        base = [(k * halves + h) * SUB for h in range(halves)]
        rows = [pl.ds(pl.multiple_of(b, SUB), SUB) for b in base]
        col = [col_ref[r, :] for r in rows]
        at = [c & (LANES - 1) for c in col]
        number = [c >> 7 for c in col]
        low = span_ref[0, k * halves]
        high = span_ref[SUB, k * halves]
        for h in range(1, halves):
            low = jnp.minimum(low, span_ref[0, k * halves + h])
            high = jnp.maximum(high, span_ref[SUB, k * halves + h])

        def block(b, values):
            values = list(values)
            for r in range(chunks):
                match = [n == b * chunks + r for n in number]
                for c in range(FIELDS):
                    row = big[b, c, r]
                    for h in range(halves):
                        found = jnp.take_along_axis(row, at[h], axis=1)
                        values[h * FIELDS + c] = jnp.where(match[h], found, values[h * FIELDS + c])
            return tuple(values)

        zeros = tuple(jnp.zeros((SUB, LANES), f32) for _ in range(FIELDS * halves))
        other = lax.fori_loop(low, high + 1, block, zeros)
        sums = list(sums)
        for h in range(halves):
            diff = [own_ref[c, h * SUB : (h + 1) * SUB, :] - other[h * FIELDS + c] for c in range(FIELDS)]
            e = [terms_ref[c, rows[h], :] for c in range(3)]
            c1 = terms_ref[3, rows[h], :]
            size = e[0] * e[0] + e[1] * e[1] + e[2] * e[2]
            c2 = c1 * (1.0 - size)
            p = e[0] * diff[0] + e[1] * diff[1] + e[2] * diff[2]
            t = e[0] * diff[3] + e[1] * diff[4] + e[2] * diff[5]
            mix = 0.8 * c1
            along_top = 6.0 * c2 * p + mix * t
            along_bottom = mix * p - 2.0 * c1 * t
            cross = mix * (size * (1.0 / 3.0))
            strong = 2.5 * c1
            for c in range(3):
                top = e[c] * along_top + c1 * diff[c] - cross * diff[3 + c]
                bottom = e[c] * along_bottom - cross * diff[c] + strong * diff[3 + c]
                sums[h * FIELDS + c] = sums[h * FIELDS + c] + top
                sums[h * FIELDS + 3 + c] = sums[h * FIELDS + 3 + c] + bottom
        return tuple(sums)

    start = []
    for h in range(halves):
        for c in range(FIELDS):
            own = own_ref[c, h * SUB : (h + 1) * SUB, :]
            start.append(drag_ref[c * chunks + h * SUB : c * chunks + (h + 1) * SUB, :] * own)
    sums = lax.fori_loop(0, K, slot, tuple(start))
    for h in range(halves):
        for c in range(FIELDS):
            out_ref[c, h * SUB : (h + 1) * SUB, :] = sums[h * FIELDS + c]


def two_sum(a, b):
    s = a + b
    t = s - a
    return s, (a - (s - t)) + (b - t)


def quick(a, b):
    s = a + b
    return s, b - (s - a)


def halve(a):
    t = a * 4097.0
    high = t - (t - a)
    return high, a - high


def two_prod(a, b, a_parts=None, b_parts=None):
    ah, al = a_parts or halve(a)
    bh, bl = b_parts or halve(b)
    p = a * b
    return p, ((ah * bh - p) + ah * bl + al * bh) + al * bl


class Pair:
    def __init__(self, high, low):
        self.high, self.low = high, low

    def __add__(self, other):
        s, e = two_sum(self.high, other.high)
        return Pair(*quick(s, e + (self.low + other.low)))

    def __neg__(self):
        return Pair(-self.high, -self.low)

    def __mul__(self, other):
        p, e = two_prod(self.high, other.high)
        return Pair(*quick(p, e + (self.high * other.low + self.low * other.high)))

    def __truediv__(self, other):
        q = self.high / other.high
        p, e = two_prod(q, other.high)
        rest = ((self.high - p) - e) + (self.low - q * other.low)
        return Pair(*quick(q, rest / other.high))


GRAM = [(a, b) for a in range(ITERS + 1) for b in range(a, ITERS + 1)]


def gram_row(vectors):
    zero = jnp.zeros((SUB, LANES), f32)
    sums = [(zero, zero) for _ in GRAM]
    fields, chunks, _ = vectors[0].shape
    for c in range(fields):
        for h in range(chunks // SUB):
            x = [v[c, h * SUB : (h + 1) * SUB, :] for v in vectors]
            parts = [halve(a) for a in x]
            for n, (a, b) in enumerate(GRAM):
                p, e = two_prod(x[a], x[b], parts[a], parts[b])
                s, rest = two_sum(sums[n][0], p)
                sums[n] = (s, sums[n][1] + (e + rest))
    lane = iota((SUB, LANES), 1)
    sub = iota((SUB, LANES), 0)
    row = zero
    for base in range(0, len(GRAM), SUB):
        packed = (zero, zero)
        for n in range(base, min(base + SUB, len(GRAM))):
            s, e = sums[n]
            for step in (4, 2, 1):
                s, rest = two_sum(s, pltpu.roll(s, step, 0))
                e = e + pltpu.roll(e, step, 0) + rest
            packed = tuple(jnp.where(sub == n - base, new, old) for new, old in zip((s, e), packed))
        s, e = packed
        for step in (64, 32, 16, 8, 4, 2, 1):
            s, rest = two_sum(s, pltpu.roll(s, step, 1))
            e = e + pltpu.roll(e, step, 1) + rest
        row = row + jnp.where(lane == sub + base, s, 0.0) + jnp.where(lane == sub + (base + 64), e, 0.0)
    return jnp.sum(row, axis=0, keepdims=True)


def gram_total(rows_ref):
    total = Pair(jnp.zeros((SUB, LANES), f32), jnp.zeros((SUB, LANES), f32))
    for n in range(rows_ref.shape[0] // SUB):
        x = rows_ref[n * SUB : (n + 1) * SUB, :]
        total = total + Pair(x, pltpu.roll(x, 64, 1))
    for step in (4, 2, 1):
        total = total + Pair(pltpu.roll(total.high, step, 0), pltpu.roll(total.low, step, 0))
    grid = {}
    for n, (a, b) in enumerate(GRAM):
        at = jnp.full((SUB, LANES), n, i32)
        grid[a, b] = grid[b, a] = Pair(*quick(*(jnp.take_along_axis(x, at, axis=1) for x in (total.high, total.low))))
    return grid


def weigh(grid, x, y, shift):
    out = None
    for i, a in enumerate(x):
        for j, b in enumerate(y):
            term = grid[i, j + shift] if a is None and b is None else None
            if term is None:
                term = grid[i, j + shift] * (a if b is None else b if a is None else a * b)
            out = term if out is None else out + term
    return out


def conjugate(grid):
    zero = jnp.zeros((SUB, LANES), f32)
    one = Pair(zero + 1.0, zero)
    c = [one]
    d = [one]
    x = []
    norm = grid[0, 0]
    least = None
    for iteration in range(ITERS):
        step = norm / weigh(grid, d, d, 1)
        x = [a + step * b if a is not None else step * b for a, b in zip(x + [None], d)]
        c = [
            (c[n] if n < len(c) else None, -(step * d[n - 1]) if n else None) for n in range(len(d) + 1)
        ]
        c = [a if b is None else b if a is None else a + b for a, b in c]
        new = weigh(grid, c, c, 0)
        least = new.high if least is None else jnp.minimum(least, new.high)
        ratio = new / norm
        d = [a + ratio * b if b is not None else a for a, b in zip(c, d + [None])]
        norm = new
    size = zero
    for n in range(ITERS + 1):
        size = size + jnp.abs(c[n].high) * jnp.sqrt(grid[n, n].high)
    return [a.high for a in x], [a.high for a in c], jnp.where(least > 1e-6 * (size * size), 1.0, 0.0)


def first_kernel(
    spheres, tab, pos, got, drag, below, mid, above, terms, col, span, drag_out, out, big, span_s, sem
):
    chunks = spheres // LANES
    place_pick(spheres, got, tab, pos, terms, col)
    place_blocks(spheres, col, span)
    copy = pltpu.make_async_copy(span, span_s, sem)
    copy.start()
    for r in range(chunks):
        drag_out[pl.ds(r, FIELDS, stride=chunks), :] = drag[:, r * LANES : (r + 1) * LANES]
    spread([below, mid, above], big)
    copy.wait()
    apply_operator(mid.at[1], big, span_s, col, terms, drag_out, out)


def next_kernel(span, col, terms, drag, below, mid, above, out, big):
    spread([below, mid, above], big)
    apply_operator(mid.at[1], big, span, col, terms, drag, out)


def third_kernel(span, col, terms, drag, below, mid, above, k0, k1, out, row_out, big):
    next_kernel(span, col, terms, drag, below, mid, above, out, big)
    row = gram_row([k0, k1, mid.at[1], out])
    row_out[...] = jnp.broadcast_to(row, row_out.shape)


def last_kernel(rows, k0, k1, k2, k3, velocity, residual, good, v_s, r_s):
    x, c, ok = conjugate(gram_total(rows))
    chunks = k0.shape[1]
    k = [k0, k1, k2, k3]
    for n in range(k0.shape[0]):
        for h in range(chunks // SUB):
            part = [a[n, h * SUB : (h + 1) * SUB, :] for a in k]
            rows_out = slice(n * chunks + h * SUB, n * chunks + (h + 1) * SUB)
            v_s[rows_out, :] = x[0] * part[0] + x[1] * part[1] + x[2] * part[2]
            r_s[rows_out, :] = part[0] + c[1] * part[1] + c[2] * part[2] + c[3] * part[3]
    for r in range(chunks):
        velocity[:, r * LANES : (r + 1) * LANES] = v_s[pl.ds(r, FIELDS, stride=chunks), :]
        residual[:, r * LANES : (r + 1) * LANES] = r_s[pl.ds(r, FIELDS, stride=chunks), :]
    good[0, 0] = jnp.min(ok).astype(i32)


VMEM = pl.BlockSpec(memory_space=pltpu.VMEM)
SMEM = pl.BlockSpec(memory_space=pltpu.SMEM)
PARAMS = pltpu.CompilerParams(vmem_limit_bytes=24 << 20)


def shape(dims, dtype=f32):
    return jax.ShapeDtypeStruct(dims, dtype)


def ring(axis, step):
    count = lax.axis_size(axis)
    return [(i, (i + step) % count) for i in range(count)]


def beside(x):
    west = lax.ppermute(x, "gx", ring("gx", 1))
    east = lax.ppermute(x, "gx", ring("gx", -1))
    mid = jnp.stack([west, x, east])
    below = lax.ppermute(mid, "gy", ring("gy", 1))
    above = lax.ppermute(mid, "gy", ring("gy", -1))
    return below, mid, above


def plain(apply, forces):
    def both(a, b):
        return lax.psum(jnp.sum(a * b), ("gx", "gy"))

    velocity = jnp.zeros_like(forces)
    residual = direction = forces
    norm = both(residual, residual)
    for iteration in range(ITERS):
        applied = apply(direction)
        step = norm / both(direction, applied)
        velocity = velocity + step * direction
        residual = residual - step * applied
        new = both(residual, residual)
        direction = residual + new / norm * direction
        norm = new
    return velocity, residual


def on_device(pair_ends, pair_geometry, drag_coef, forces):
    spheres = drag_coef.shape[1]
    chunks = spheres // LANES
    slabs = lax.axis_size("gx")
    devices = slabs * lax.axis_size("gy")
    field = (FIELDS, chunks, LANES)
    slot_rows = K * spheres // LANES
    big = pltpu.VMEM((9, FIELDS, chunks, SUB, LANES), f32)
    labels, values, k0 = pack(pair_ends, pair_geometry, forces, slabs, lax.axis_size("gy"))
    got_labels = lax.all_to_all(labels, "gx", split_axis=0, concat_axis=0, tiled=True)
    got = lax.all_to_all(values, "gx", split_axis=0, concat_axis=0, tiled=True)
    k0 = k0.reshape(field)
    near = beside(k0)
    pos, tab = invert(got_labels, spheres)
    terms, col, span, drag, k1 = pl.pallas_call(
        functools.partial(first_kernel, spheres),
        out_shape=(
            shape((SENT - 2, slot_rows, LANES)),
            shape((slot_rows, LANES), i32),
            shape((2 * SUB, LANES), i32),
            shape((FIELDS * chunks, LANES)),
            shape(field),
        ),
        in_specs=[SMEM] + [VMEM] * 6,
        scratch_shapes=[big, pltpu.SMEM((2 * SUB, LANES), i32), pltpu.SemaphoreType.DMA],
        compiler_params=PARAMS,
        name="first",
    )(tab, pos, got, drag_coef, *near)

    def apply(x):
        return pl.pallas_call(
            next_kernel,
            out_shape=shape(field),
            in_specs=[SMEM] + [VMEM] * 6,
            scratch_shapes=[big],
            compiler_params=PARAMS,
            name="next",
        )(span, col, terms, drag, *beside(x))

    k2 = apply(k1)
    k3, rows = pl.pallas_call(
        third_kernel,
        out_shape=(shape(field), shape((devices, LANES))),
        in_specs=[SMEM] + [VMEM] * 8,
        scratch_shapes=[big],
        compiler_params=PARAMS,
        name="third",
    )(span, col, terms, drag, *beside(k2), k0, k1)
    rows = lax.all_to_all(rows, ("gx", "gy"), split_axis=0, concat_axis=0, tiled=True)
    velocity, residual, good = pl.pallas_call(
        last_kernel,
        out_shape=(shape((FIELDS, spheres)), shape((FIELDS, spheres)), shape((1, 1), i32)),
        out_specs=(VMEM, VMEM, SMEM),
        scratch_shapes=[pltpu.VMEM((FIELDS * chunks, LANES), f32)] * 2,
        compiler_params=PARAMS,
        name="last",
    )(rows, k0, k1, k2, k3)

    def again(results):
        v, r = plain(apply, k0)
        return v.reshape(FIELDS, spheres), r.reshape(FIELDS, spheres)

    return lax.cond(good[0, 0] > 0, lambda results: results, again, (velocity, residual))


def solution(mesh):
    spec = P(None, ("gx", "gy"))
    return jax.shard_map(
        on_device, mesh=mesh, in_specs=(spec,) * 4, out_specs=(spec, spec), check_vma=False
    )
```

```python
import functools

import jax
import jax.numpy as jnp
from jax import lax
from jax.experimental import pallas as pl
from jax.experimental.pallas import tpu as pltpu
from jax.sharding import PartitionSpec as P

K = 16
ITERS = 3
LANES = 128
SUB = 8
FIELDS = 6
SENT = 6
TILE = SUB * LANES

f32 = jnp.float32
i32 = jnp.int32
bf16 = jnp.bfloat16


def log2(n):
    assert n & (n - 1) == 0
    return n.bit_length() - 1


def iota(shape, dim):
    return lax.broadcasted_iota(i32, shape, dim)


def pack_kernel(slabs, strips, spheres, ends_ref, geo_ref, force_ref, send_ref, dense_ref, ends_s, geo_s, out_s):
    rows = ends_ref.shape[1] // LANES
    padded = ends_s.shape[0] // 3
    cap_rows = send_ref.shape[2]
    chunks = spheres // LANES
    for r in range(rows):
        cols = slice(r * LANES, (r + 1) * LANES)
        ends_s[pl.ds(r, 3, stride=padded), :] = ends_ref[:, cols]
        geo_s[pl.ds(r, 5, stride=padded), :] = geo_ref[:, cols]
    for r in range(chunks):
        dense_ref[pl.ds(r, FIELDS, stride=chunks), :] = force_ref[:, r * LANES : (r + 1) * LANES]
    first = ends_s[0:padded, :]
    second = ends_s[padded : 2 * padded, :]
    slot = ends_s[2 * padded : 3 * padded, :]
    inside = iota((padded, LANES), 0) < rows
    live = jnp.logical_and(slot < K, inside)
    shift = log2(spheres)
    first_block = first >> shift
    second_block = second >> shift
    owner = first_block >> log2(strips)
    shift_x = ((second_block >> log2(strips)) - owner + 1) & (slabs - 1)
    shift_y = ((second_block & (strips - 1)) - (first_block & (strips - 1)) + 1) & (strips - 1)
    column = (shift_y * 3 + shift_x) * spheres + (second & (spheres - 1))
    place = first & (spheres - 1)
    tile = slot * (spheres // TILE) + (place >> log2(TILE))
    target = ((place & (LANES - 1)) * SUB + ((place >> log2(LANES)) & (SUB - 1))) * (K * spheres // TILE) + tile
    owner = jnp.where(live, owner, slabs)
    sep = [geo_s[c * padded : (c + 1) * padded, :] for c in range(3)]
    a = geo_s[3 * padded : 4 * padded, :]
    b = geo_s[4 * padded : 5 * padded, :]
    h = a + b
    total = sep[0] * sep[0] + sep[1] * sep[1] + sep[2] * sep[2] + h * h
    inv = lax.rsqrt(total)
    values = [target.astype(f32), column.astype(f32)] + [d * inv for d in sep] + [a * b * h * (inv * inv)]
    for c, value in enumerate(values):
        out_s[c, 0:padded, :] = value
    lane = iota((cap_rows, LANES), 1)
    place = iota((cap_rows, LANES), 0) * LANES + lane
    start = jnp.int32(0)
    for o in range(slabs):
        end = jnp.sum(jnp.where(owner <= o, 1.0, 0.0)).astype(i32)
        row = start >> 7
        off = start & (LANES - 1)
        back = (LANES - off) & (LANES - 1)
        for c in range(SENT):
            here = pltpu.roll(out_s[c, pl.ds(row, cap_rows), :], back, 1)
            after = pltpu.roll(out_s[c, pl.ds(row + 1, cap_rows), :], back, 1)
            value = jnp.where(lane < LANES - off, here, after)
            if c == 0:
                value = jnp.where(place < end - start, value, -1.0)
            send_ref[o, c] = value
        start = end


def pack(ends, geo, forces, slabs, strips):
    spheres = forces.shape[1]
    cap_rows = spheres * K // slabs // LANES
    rows = ends.shape[1] // LANES
    padded = -(-rows // SUB) * SUB
    return pl.pallas_call(
        functools.partial(pack_kernel, slabs, strips, spheres),
        out_shape=(
            jax.ShapeDtypeStruct((slabs, SENT, cap_rows, LANES), f32),
            jax.ShapeDtypeStruct((FIELDS * spheres // LANES, LANES), f32),
        ),
        scratch_shapes=[
            pltpu.VMEM((3 * padded, LANES), i32),
            pltpu.VMEM((5 * padded, LANES), f32),
            pltpu.VMEM((SENT, padded + cap_rows + SUB, LANES), f32),
        ],
        name="pack",
    )(ends, geo, forces)


def place_ranges(got_ref, tab_v):
    sources, _, cap_rows, _ = got_ref.shape
    tiles = sources * cap_rows // SUB
    lane = iota((SUB, LANES), 1)
    lane_f = lane.astype(f32)
    big = float(1 << 20)
    for group in range(sources // SUB):
        low = jnp.full((SUB, LANES), big, f32)
        high = jnp.full((SUB, LANES), -1.0, f32)
        for k in range(cap_rows):
            t = got_ref[group * SUB : (group + 1) * SUB, 0, k, :]
            tile = t - float(tiles) * jnp.floor(t * (1.0 / tiles))
            t_low = jnp.min(jnp.where(t < 0.0, big, tile), axis=1, keepdims=True)
            t_high = jnp.max(jnp.where(t < 0.0, -1.0, tile), axis=1, keepdims=True)
            low = jnp.where(lane == k, t_low, low)
            high = jnp.where(lane == k, t_high, high)
        starts = jnp.zeros((SUB, LANES), f32)
        counts = jnp.zeros((SUB, LANES), f32)
        for q in range(tiles):
            hit = jnp.logical_and(low <= q, high >= q)
            k_low = jnp.min(jnp.where(hit, lane_f, float(cap_rows - 1)), axis=1, keepdims=True)
            k_high = jnp.max(jnp.where(hit, lane_f, -1.0), axis=1, keepdims=True)
            starts = jnp.where(lane == q, k_low, starts)
            counts = jnp.where(lane == q, k_high - k_low + 1.0, counts)
        tab_v[group, 0] = starts.astype(i32)
        tab_v[group, 1] = jnp.broadcast_to(jnp.max(counts, axis=0, keepdims=True), (SUB, LANES)).astype(i32)


def place_sort(got_ref, pos_ref):
    sources, _, cap_rows, _ = got_ref.shape
    tiles = sources * cap_rows // SUB
    dims = (tiles, SUB, LANES)
    tile_bits, sub_bits = log2(tiles), log2(SUB)
    bits = log2(tiles * TILE)
    empty = 1 << (2 * bits)
    t = got_ref[:, 0].reshape(dims).astype(i32)
    home = (iota(dims, 0) * SUB + iota(dims, 1)) * LANES + iota(dims, 2)
    x = jnp.where(t < 0, empty, t << bits) + home
    place = (iota(dims, 2) * SUB + iota(dims, 1)) * tiles + iota(dims, 0)

    def partner(x, bit):
        axis, size, d = (1, SUB, 1 << (bit - tile_bits)) if bit < tile_bits + sub_bits else (
            2, LANES, 1 << (bit - tile_bits - sub_bits))
        if 2 * d == size:
            return pltpu.roll(x, d, axis)
        upper = (iota(dims, axis) & d) != 0
        return jnp.where(upper, pltpu.roll(x, d, axis), pltpu.roll(x, size - d, axis))

    def exchange(x, bit):
        if bit < tile_bits:
            pairs = x.reshape((tiles >> (bit + 1), 2, 1 << bit, SUB, LANES))
            low = jnp.minimum(pairs[:, 0:1], pairs[:, 1:2])
            high = jnp.maximum(pairs[:, 0:1], pairs[:, 1:2])
            return jnp.concatenate([low, high], axis=1).reshape(dims)
        other = partner(x, bit)
        upper = (place & (1 << bit)) != 0
        return jnp.where(jnp.logical_xor(x < other, upper), x, other)

    for m in range(1, bits + 1):
        flip = -(((place >> m) ^ (place >> (m - 1) if m > 1 else 0)) & 1)
        x = x ^ flip
        for bit in range(m - 1, -1, -1):
            x = exchange(x, bit)

    def carry(x):
        x = pltpu.roll(x, 1, 1)
        return jnp.where(iota(x.shape, 1) < 1, pltpu.roll(x, 1, 2), x)

    for bit in range(bits - 1, -1, -1):
        move = jnp.logical_and(x < empty, x - (place << bits) >= (1 << (bit + bits)))
        y = jnp.where(move, x, empty)
        x = jnp.where(move, empty, x)
        if bit < tile_bits:
            d = 1 << bit
            y = jnp.concatenate([carry(y[tiles - d :]), y[: tiles - d]], axis=0)
        elif bit < tile_bits + sub_bits:
            d = 1 << (bit - tile_bits)
            y = pltpu.roll(y, d, 1)
            y = jnp.where(iota(dims, 1) < d, pltpu.roll(y, 1, 2), y)
        else:
            y = pltpu.roll(y, 1 << (bit - tile_bits - sub_bits), 2)
        x = jnp.minimum(x, y)
    pos_ref[...] = jnp.where(x < empty, x & ((1 << bits) - 1), -1)


def place_pick(spheres, got_ref, tab_s, pos_ref, terms_ref, col_ref):
    sources, _, cap_rows, _ = got_ref.shape

    def place(q, carry):
        rows = pl.ds(pl.multiple_of(q * SUB, SUB), SUB)
        pos = pos_ref[q]
        number = pos >> log2(LANES)
        at = pos & (LANES - 1)
        values = tuple(jnp.zeros((SUB, LANES), f32) for _ in range(SENT - 1))
        for group in range(sources // SUB):

            def pick(kk, values):
                values = list(values)
                for u in range(SUB):
                    s = group * SUB + u
                    k = jnp.minimum(tab_s[group, 0, u, q] + kk, cap_rows - 1)
                    match = number == s * cap_rows + k
                    for c in range(1, SENT):
                        row = jnp.broadcast_to(got_ref[s, c, pl.ds(k, 1), :], (SUB, LANES))
                        found = jnp.take_along_axis(row, at, axis=1)
                        values[c - 1] = jnp.where(match, found, values[c - 1])
                return tuple(values)

            values = lax.fori_loop(0, tab_s[group, 1, 0, q], pick, values)
        col_ref[rows, :] = jnp.where(pos >= 0, values[0], -1.0).astype(i32)
        for c in range(SENT - 2):
            terms_ref[c, rows, :] = values[c + 1]
        return carry

    lax.fori_loop(0, K * spheres // TILE, place, 0)


def place_blocks(spheres, col_ref, span_ref):
    lane = iota((SUB, LANES), 1)
    big = float(1 << 20)
    low = jnp.full((SUB, LANES), big, f32)
    high = jnp.full((SUB, LANES), -1.0, f32)
    for q in range(K * spheres // (SUB * LANES)):
        block = (col_ref[q * SUB : (q + 1) * SUB, :] >> log2(spheres)).astype(f32)
        b_low = jnp.min(jnp.where(block < 0.0, big, block), axis=1, keepdims=True)
        b_high = jnp.max(block, axis=1, keepdims=True)
        low = jnp.where(lane == q, b_low, low)
        high = jnp.where(lane == q, b_high, high)
    span_ref[0:SUB, :] = jnp.broadcast_to(jnp.min(low, axis=0, keepdims=True), (SUB, LANES)).astype(i32)
    span_ref[SUB : 2 * SUB, :] = jnp.broadcast_to(jnp.max(high, axis=0, keepdims=True), (SUB, LANES)).astype(i32)


def gather_blocks(parts, table):
    for y, part in enumerate(parts):
        for x in range(3):
            table[3 * y + x] = part[x]


def apply_operator(table, span_ref, col_ref, terms_ref, drag_ref, out_ref):
    own_ref = table.at[4]
    chunks = table.shape[2]
    halves = chunks // SUB

    def slot(k, sums):
        base = [(k * halves + h) * SUB for h in range(halves)]
        rows = [pl.ds(pl.multiple_of(b, SUB), SUB) for b in base]
        col = [col_ref[r, :] for r in rows]
        at = [c & (LANES - 1) for c in col]
        number = [c >> 7 for c in col]
        low = span_ref[0, k * halves]
        high = span_ref[SUB, k * halves]
        for h in range(1, halves):
            low = jnp.minimum(low, span_ref[0, k * halves + h])
            high = jnp.maximum(high, span_ref[SUB, k * halves + h])

        def block(b, values):
            values = list(values)
            for r in range(chunks):
                match = [n == b * chunks + r for n in number]
                for c in range(FIELDS):
                    row = jnp.broadcast_to(table[b, c, r : r + 1, :], (SUB, LANES))
                    for h in range(halves):
                        found = jnp.take_along_axis(row, at[h], axis=1)
                        values[h * FIELDS + c] = jnp.where(match[h], found, values[h * FIELDS + c])
            return tuple(values)

        zeros = tuple(jnp.zeros((SUB, LANES), f32) for _ in range(FIELDS * halves))
        other = lax.fori_loop(low, high + 1, block, zeros)
        sums = list(sums)
        for h in range(halves):
            diff = [own_ref[c, h * SUB : (h + 1) * SUB, :] - other[h * FIELDS + c] for c in range(FIELDS)]
            e = [terms_ref[c, rows[h], :] for c in range(3)]
            c1 = terms_ref[3, rows[h], :]
            size = e[0] * e[0] + e[1] * e[1] + e[2] * e[2]
            c2 = c1 * (1.0 - size)
            p = e[0] * diff[0] + e[1] * diff[1] + e[2] * diff[2]
            t = e[0] * diff[3] + e[1] * diff[4] + e[2] * diff[5]
            mix = 0.8 * c1
            along_top = 6.0 * c2 * p + mix * t
            along_bottom = mix * p - 2.0 * c1 * t
            cross = mix * (size * (1.0 / 3.0))
            strong = 2.5 * c1
            for c in range(3):
                top = e[c] * along_top + c1 * diff[c] - cross * diff[3 + c]
                bottom = e[c] * along_bottom - cross * diff[c] + strong * diff[3 + c]
                sums[h * FIELDS + c] = sums[h * FIELDS + c] + top
                sums[h * FIELDS + 3 + c] = sums[h * FIELDS + 3 + c] + bottom
        return tuple(sums)

    start = []
    for h in range(halves):
        for c in range(FIELDS):
            own = own_ref[c, h * SUB : (h + 1) * SUB, :]
            start.append(drag_ref[c * chunks + h * SUB : c * chunks + (h + 1) * SUB, :] * own)
    sums = lax.fori_loop(0, K, slot, tuple(start))
    for h in range(halves):
        for c in range(FIELDS):
            out_ref[c, h * SUB : (h + 1) * SUB, :] = sums[h * FIELDS + c]


def two_sum(a, b):
    s = a + b
    t = s - a
    return s, (a - (s - t)) + (b - t)


def quick(a, b):
    s = a + b
    return s, b - (s - a)


def halve(a):
    t = a * 4097.0
    high = t - (t - a)
    return high, a - high


def two_prod(a, b, a_parts=None, b_parts=None):
    ah, al = a_parts or halve(a)
    bh, bl = b_parts or halve(b)
    p = a * b
    return p, ((ah * bh - p) + ah * bl + al * bh) + al * bl


class Pair:
    def __init__(self, high, low):
        self.high, self.low = high, low

    def __add__(self, other):
        s, e = two_sum(self.high, other.high)
        return Pair(*quick(s, e + (self.low + other.low)))

    def __neg__(self):
        return Pair(-self.high, -self.low)

    def __mul__(self, other):
        p, e = two_prod(self.high, other.high)
        return Pair(*quick(p, e + (self.high * other.low + self.low * other.high)))

    def __truediv__(self, other):
        q = self.high / other.high
        p, e = two_prod(q, other.high)
        rest = ((self.high - p) - e) + (self.low - q * other.low)
        return Pair(*quick(q, rest / other.high))


GRAM = [(a, b) for a in range(ITERS + 1) for b in range(a, ITERS + 1)]


def gram_row(vectors):
    zero = jnp.zeros((SUB, LANES), f32)
    sums = [(zero, zero) for _ in GRAM]
    fields, chunks, _ = vectors[0].shape
    for c in range(fields):
        for h in range(chunks // SUB):
            x = [v[c, h * SUB : (h + 1) * SUB, :] for v in vectors]
            parts = [halve(a) for a in x]
            for n, (a, b) in enumerate(GRAM):
                p, e = two_prod(x[a], x[b], parts[a], parts[b])
                s, rest = two_sum(sums[n][0], p)
                sums[n] = (s, sums[n][1] + (e + rest))
    lane = iota((SUB, LANES), 1)
    sub = iota((SUB, LANES), 0)
    row = zero
    for base in range(0, len(GRAM), SUB):
        packed = (zero, zero)
        for n in range(base, min(base + SUB, len(GRAM))):
            s, e = sums[n]
            for step in (4, 2, 1):
                s, rest = two_sum(s, pltpu.roll(s, step, 0))
                e = e + pltpu.roll(e, step, 0) + rest
            packed = tuple(jnp.where(sub == n - base, new, old) for new, old in zip((s, e), packed))
        s, e = packed
        for step in (64, 32, 16, 8, 4, 2, 1):
            s, rest = two_sum(s, pltpu.roll(s, step, 1))
            e = e + pltpu.roll(e, step, 1) + rest
        row = row + jnp.where(lane == sub + base, s, 0.0) + jnp.where(lane == sub + (base + 64), e, 0.0)
    return jnp.sum(row, axis=0, keepdims=True)


def gram_total(rows_ref):
    total = Pair(jnp.zeros((SUB, LANES), f32), jnp.zeros((SUB, LANES), f32))
    for n in range(rows_ref.shape[0] // SUB):
        x = rows_ref[n * SUB : (n + 1) * SUB, :]
        total = total + Pair(x, pltpu.roll(x, 64, 1))
    for step in (4, 2, 1):
        total = total + Pair(pltpu.roll(total.high, step, 0), pltpu.roll(total.low, step, 0))
    grid = {}
    for n, (a, b) in enumerate(GRAM):
        at = jnp.full((SUB, LANES), n, i32)
        grid[a, b] = grid[b, a] = Pair(*quick(*(jnp.take_along_axis(x, at, axis=1) for x in (total.high, total.low))))
    return grid


def weigh(grid, x, y, shift):
    out = None
    for i, a in enumerate(x):
        for j, b in enumerate(y):
            term = grid[i, j + shift] if a is None and b is None else None
            if term is None:
                term = grid[i, j + shift] * (a if b is None else b if a is None else a * b)
            out = term if out is None else out + term
    return out


def conjugate(grid):
    zero = jnp.zeros((SUB, LANES), f32)
    one = Pair(zero + 1.0, zero)
    c = [one]
    d = [one]
    x = []
    norm = grid[0, 0]
    least = None
    for iteration in range(ITERS):
        step = norm / weigh(grid, d, d, 1)
        x = [a + step * b if a is not None else step * b for a, b in zip(x + [None], d)]
        c = [
            (c[n] if n < len(c) else None, -(step * d[n - 1]) if n else None) for n in range(len(d) + 1)
        ]
        c = [a if b is None else b if a is None else a + b for a, b in c]
        new = weigh(grid, c, c, 0)
        least = new.high if least is None else jnp.minimum(least, new.high)
        ratio = new / norm
        d = [a + ratio * b if b is not None else a for a, b in zip(c, d + [None])]
        norm = new
    size = zero
    for n in range(ITERS + 1):
        size = size + jnp.abs(c[n].high) * jnp.sqrt(grid[n, n].high)
    return [a.high for a in x], [a.high for a in c], jnp.where(least > 1e-6 * (size * size), 1.0, 0.0)


def first_kernel(
    spheres, got, drag, below, mid, above, terms, col, span, drag_out, out, table, pos, tab, tab_s, span_s, sem
):
    chunks = spheres // LANES
    place_ranges(got, tab)
    copy = pltpu.make_async_copy(tab, tab_s, sem)
    copy.start()
    for r in range(chunks):
        drag_out[pl.ds(r, FIELDS, stride=chunks), :] = drag[:, r * LANES : (r + 1) * LANES]
    gather_blocks([below, mid, above], table)
    place_sort(got, pos)
    copy.wait()
    place_pick(spheres, got, tab_s, pos, terms, col)
    place_blocks(spheres, col, span)
    copy = pltpu.make_async_copy(span, span_s, sem)
    copy.start()
    copy.wait()
    apply_operator(table, span_s, col, terms, drag_out, out)


def next_kernel(span, col, terms, drag, below, mid, above, out, table):
    gather_blocks([below, mid, above], table)
    apply_operator(table, span, col, terms, drag, out)


def third_kernel(span, col, terms, drag, below, mid, above, k0, k1, out, row_out, table):
    next_kernel(span, col, terms, drag, below, mid, above, out, table)
    row = gram_row([k0, k1, mid.at[1], out])
    row_out[...] = jnp.broadcast_to(row, row_out.shape)


def last_kernel(rows, k0, k1, k2, k3, velocity, residual, good, dense, flat, sem):
    x, c, ok = conjugate(gram_total(rows))
    chunks = k0.shape[1]
    k = [k0, k1, k2, k3]
    for n in range(k0.shape[0]):
        for h in range(chunks // SUB):
            part = [a[n, h * SUB : (h + 1) * SUB, :] for a in k]
            here = slice(n * chunks + h * SUB, n * chunks + (h + 1) * SUB)
            dense[0, here, :] = x[0] * part[0] + x[1] * part[1] + x[2] * part[2]
            dense[1, here, :] = part[0] + c[1] * part[1] + c[2] * part[2] + c[3] * part[3]
    copies = []
    for out, target in enumerate((velocity, residual)):
        for r in range(chunks):
            flat[out, :, r * LANES : (r + 1) * LANES] = dense[out, pl.ds(r, FIELDS, stride=chunks), :]
        copies.append(pltpu.make_async_copy(flat.at[out], target, sem.at[out]))
        copies[-1].start()
    good[0, 0] = jnp.min(ok).astype(i32)
    for copy in copies:
        copy.wait()


VMEM = pl.BlockSpec(memory_space=pltpu.VMEM)
SMEM = pl.BlockSpec(memory_space=pltpu.SMEM)
HBM = pl.BlockSpec(memory_space=pltpu.HBM)
PARAMS = pltpu.CompilerParams(vmem_limit_bytes=24 << 20)


def shape(dims, dtype=f32):
    return jax.ShapeDtypeStruct(dims, dtype)


def ring(axis, step):
    count = lax.axis_size(axis)
    return [(i, (i + step) % count) for i in range(count)]


def beside(x):
    west = lax.ppermute(x, "gx", ring("gx", 1))
    east = lax.ppermute(x, "gx", ring("gx", -1))
    mid = jnp.stack([west, x, east])
    below = lax.ppermute(mid, "gy", ring("gy", 1))
    above = lax.ppermute(mid, "gy", ring("gy", -1))
    return below, mid, above


def plain(apply, forces):
    def both(a, b):
        return lax.psum(jnp.sum(a * b), ("gx", "gy"))

    velocity = jnp.zeros_like(forces)
    residual = direction = forces
    norm = both(residual, residual)
    for iteration in range(ITERS):
        applied = apply(direction)
        step = norm / both(direction, applied)
        velocity = velocity + step * direction
        residual = residual - step * applied
        new = both(residual, residual)
        direction = residual + new / norm * direction
        norm = new
    return velocity, residual


def on_device(pair_ends, pair_geometry, drag_coef, forces):
    spheres = drag_coef.shape[1]
    chunks = spheres // LANES
    slabs = lax.axis_size("gx")
    devices = slabs * lax.axis_size("gy")
    field = (FIELDS, chunks, LANES)
    slot_rows = K * spheres // LANES
    table = pltpu.VMEM((9, FIELDS, chunks, LANES), f32)
    ranges = (slabs // SUB, 2, SUB, LANES)
    assert K * spheres == SUB * 4 * TILE and slabs % SUB == 0
    send, k0 = pack(pair_ends, pair_geometry, forces, slabs, lax.axis_size("gy"))
    got = lax.all_to_all(send, "gx", split_axis=0, concat_axis=0, tiled=True)
    k0 = k0.reshape(field)
    terms, col, span, drag, k1 = pl.pallas_call(
        functools.partial(first_kernel, spheres),
        out_shape=(
            shape((SENT - 2, slot_rows, LANES)),
            shape((slot_rows, LANES), i32),
            shape((2 * SUB, LANES), i32),
            shape((FIELDS * chunks, LANES)),
            shape(field),
        ),
        in_specs=[VMEM] * 5,
        scratch_shapes=[
            table,
            pltpu.VMEM((slot_rows // SUB, SUB, LANES), i32),
            pltpu.VMEM(ranges, i32),
            pltpu.SMEM(ranges, i32),
            pltpu.SMEM((2 * SUB, LANES), i32),
            pltpu.SemaphoreType.DMA,
        ],
        compiler_params=PARAMS,
        name="first",
    )(got, drag_coef, *beside(k0))

    def apply(x):
        return pl.pallas_call(
            next_kernel,
            out_shape=shape(field),
            in_specs=[SMEM] + [VMEM] * 6,
            scratch_shapes=[table],
            compiler_params=PARAMS,
            name="next",
        )(span, col, terms, drag, *beside(x))

    k2 = apply(k1)
    k3, rows = pl.pallas_call(
        third_kernel,
        out_shape=(shape(field), shape((devices, LANES))),
        in_specs=[SMEM] + [VMEM] * 8,
        scratch_shapes=[table],
        compiler_params=PARAMS,
        name="third",
    )(span, col, terms, drag, *beside(k2), k0, k1)
    rows = lax.all_to_all(rows, ("gx", "gy"), split_axis=0, concat_axis=0, tiled=True)
    velocity, residual, good = pl.pallas_call(
        last_kernel,
        out_shape=(shape((FIELDS, spheres)), shape((FIELDS, spheres)), shape((1, 1), i32)),
        out_specs=(HBM, HBM, SMEM),
        scratch_shapes=[
            pltpu.VMEM((2, FIELDS * chunks, LANES), f32),
            pltpu.VMEM((2, FIELDS, spheres), f32),
            pltpu.SemaphoreType.DMA((2,)),
        ],
        compiler_params=PARAMS,
        name="last",
    )(rows, k0, k1, k2, k3)

    def again(state):
        v, r = plain(apply, k0)
        return jnp.ones_like(good), v.reshape(FIELDS, spheres), r.reshape(FIELDS, spheres)

    return lax.while_loop(lambda state: state[0][0, 0] == 0, again, (good, velocity, residual))[1:]


def solution(mesh):
    spec = P(None, ("gx", "gy"))
    return jax.shard_map(
        on_device, mesh=mesh, in_specs=(spec,) * 4, out_specs=(spec, spec), check_vma=False
    )
```

```python
import functools

import jax
import jax.numpy as jnp
from jax import lax
from jax.experimental import pallas as pl
from jax.experimental.pallas import tpu as pltpu
from jax.sharding import PartitionSpec as P

K = 16
ITERS = 3
LANES = 128
SUB = 8
FIELDS = 6
SENT = 6
TILE = SUB * LANES

f32 = jnp.float32
i32 = jnp.int32
bf16 = jnp.bfloat16


def log2(n):
    assert n & (n - 1) == 0
    return n.bit_length() - 1


def iota(shape, dim):
    return lax.broadcasted_iota(i32, shape, dim)


def pack_kernel(slabs, strips, spheres, ends_ref, geo_ref, force_ref, send_ref, dense_ref, ends_s, geo_s, out_s):
    rows = ends_ref.shape[1] // LANES
    padded = ends_s.shape[0] // 3
    cap_rows = send_ref.shape[2]
    chunks = spheres // LANES
    for r in range(rows):
        cols = slice(r * LANES, (r + 1) * LANES)
        ends_s[pl.ds(r, 3, stride=padded), :] = ends_ref[:, cols]
        geo_s[pl.ds(r, 5, stride=padded), :] = geo_ref[:, cols]
    for r in range(chunks):
        dense_ref[pl.ds(r, FIELDS, stride=chunks), :] = force_ref[:, r * LANES : (r + 1) * LANES]
    first = ends_s[0:padded, :]
    second = ends_s[padded : 2 * padded, :]
    slot = ends_s[2 * padded : 3 * padded, :]
    inside = iota((padded, LANES), 0) < rows
    live = jnp.logical_and(slot < K, inside)
    shift = log2(spheres)
    first_block = first >> shift
    second_block = second >> shift
    owner = first_block >> log2(strips)
    shift_x = ((second_block >> log2(strips)) - owner + 1) & (slabs - 1)
    shift_y = ((second_block & (strips - 1)) - (first_block & (strips - 1)) + 1) & (strips - 1)
    column = (shift_y * 3 + shift_x) * spheres + (second & (spheres - 1))
    place = first & (spheres - 1)
    tile = slot * (spheres // TILE) + (place >> log2(TILE))
    target = ((place & (LANES - 1)) * SUB + ((place >> log2(LANES)) & (SUB - 1))) * (K * spheres // TILE) + tile
    owner = jnp.where(live, owner, slabs)
    sep = [geo_s[c * padded : (c + 1) * padded, :] for c in range(3)]
    a = geo_s[3 * padded : 4 * padded, :]
    b = geo_s[4 * padded : 5 * padded, :]
    h = a + b
    total = sep[0] * sep[0] + sep[1] * sep[1] + sep[2] * sep[2] + h * h
    inv = lax.rsqrt(total)
    values = [target.astype(f32), column.astype(f32)] + [d * inv for d in sep] + [a * b * h * (inv * inv)]
    for c, value in enumerate(values):
        out_s[c, 0:padded, :] = value
    lane = iota((cap_rows, LANES), 1)
    place = iota((cap_rows, LANES), 0) * LANES + lane
    ends = [jnp.sum(jnp.where(owner <= o, 1.0, 0.0)).astype(i32) for o in range(slabs)]
    start = jnp.int32(0)
    for o in range(slabs):
        end = ends[o]
        row = start >> 7
        off = start & (LANES - 1)
        back = (LANES - off) & (LANES - 1)
        for c in range(SENT):
            here = pltpu.roll(out_s[c, pl.ds(row, cap_rows), :], back, 1)
            after = pltpu.roll(out_s[c, pl.ds(row + 1, cap_rows), :], back, 1)
            value = jnp.where(lane < LANES - off, here, after)
            if c == 0:
                value = jnp.where(place < end - start, value, -1.0)
            send_ref[o, c] = value
        start = end


def pack(ends, geo, forces, slabs, strips):
    spheres = forces.shape[1]
    cap_rows = spheres * K // slabs // LANES
    rows = ends.shape[1] // LANES
    padded = -(-rows // SUB) * SUB
    return pl.pallas_call(
        functools.partial(pack_kernel, slabs, strips, spheres),
        out_shape=(
            jax.ShapeDtypeStruct((slabs, SENT, cap_rows, LANES), f32),
            jax.ShapeDtypeStruct((FIELDS * spheres // LANES, LANES), f32),
        ),
        scratch_shapes=[
            pltpu.VMEM((3 * padded, LANES), i32),
            pltpu.VMEM((5 * padded, LANES), f32),
            pltpu.VMEM((SENT, padded + cap_rows + SUB, LANES), f32),
        ],
        name="pack",
    )(ends, geo, forces)


def place_ranges(got_ref, tab_v):
    sources, _, cap_rows, _ = got_ref.shape
    tiles = sources * cap_rows // SUB
    lane = iota((SUB, LANES), 1)
    lane_f = lane.astype(f32)
    big = float(1 << 20)
    for group in range(sources // SUB):
        low = jnp.full((SUB, LANES), big, f32)
        high = jnp.full((SUB, LANES), -1.0, f32)
        for k in range(cap_rows):
            t = got_ref[group * SUB : (group + 1) * SUB, 0, k, :]
            tile = t - float(tiles) * jnp.floor(t * (1.0 / tiles))
            t_low = jnp.min(jnp.where(t < 0.0, big, tile), axis=1, keepdims=True)
            t_high = jnp.max(jnp.where(t < 0.0, -1.0, tile), axis=1, keepdims=True)
            low = jnp.where(lane == k, t_low, low)
            high = jnp.where(lane == k, t_high, high)
        starts = jnp.zeros((SUB, LANES), f32)
        counts = jnp.zeros((SUB, LANES), f32)
        for q in range(tiles):
            hit = jnp.logical_and(low <= q, high >= q)
            k_low = jnp.min(jnp.where(hit, lane_f, float(cap_rows - 1)), axis=1, keepdims=True)
            k_high = jnp.max(jnp.where(hit, lane_f, -1.0), axis=1, keepdims=True)
            starts = jnp.where(lane == q, k_low, starts)
            counts = jnp.where(lane == q, k_high - k_low + 1.0, counts)
        tab_v[group, 0] = starts.astype(i32)
        tab_v[group, 1] = jnp.broadcast_to(jnp.max(counts, axis=0, keepdims=True), (SUB, LANES)).astype(i32)


def place_sort(got_ref, pos_ref):
    sources, _, cap_rows, _ = got_ref.shape
    tiles = sources * cap_rows // SUB
    dims = (tiles, SUB, LANES)
    tile_bits, sub_bits = log2(tiles), log2(SUB)
    bits = log2(tiles * TILE)
    empty = 1 << (2 * bits)
    t = got_ref[:, 0].reshape(dims).astype(i32)
    home = (iota(dims, 0) * SUB + iota(dims, 1)) * LANES + iota(dims, 2)
    x = jnp.where(t < 0, empty, t << bits) + home
    place = (iota(dims, 2) * SUB + iota(dims, 1)) * tiles + iota(dims, 0)

    def partner(x, bit):
        axis, size, d = (1, SUB, 1 << (bit - tile_bits)) if bit < tile_bits + sub_bits else (
            2, LANES, 1 << (bit - tile_bits - sub_bits))
        if 2 * d == size:
            return pltpu.roll(x, d, axis)
        upper = (iota(dims, axis) & d) != 0
        return jnp.where(upper, pltpu.roll(x, d, axis), pltpu.roll(x, size - d, axis))

    def exchange(x, bit):
        if bit < tile_bits:
            pairs = x.reshape((tiles >> (bit + 1), 2, 1 << bit, SUB, LANES))
            low = jnp.minimum(pairs[:, 0:1], pairs[:, 1:2])
            high = jnp.maximum(pairs[:, 0:1], pairs[:, 1:2])
            return jnp.concatenate([low, high], axis=1).reshape(dims)
        other = partner(x, bit)
        upper = (place & (1 << bit)) != 0
        return jnp.where(jnp.logical_xor(x < other, upper), x, other)

    for m in range(1, bits + 1):
        flip = -(((place >> m) ^ (place >> (m - 1) if m > 1 else 0)) & 1)
        x = x ^ flip
        for bit in range(m - 1, -1, -1):
            x = exchange(x, bit)

    def carry(x):
        x = pltpu.roll(x, 1, 1)
        return jnp.where(iota(x.shape, 1) < 1, pltpu.roll(x, 1, 2), x)

    for bit in range(bits - 1, -1, -1):
        move = jnp.logical_and(x < empty, x - (place << bits) >= (1 << (bit + bits)))
        y = jnp.where(move, x, empty)
        x = jnp.where(move, empty, x)
        if bit < tile_bits:
            d = 1 << bit
            y = jnp.concatenate([carry(y[tiles - d :]), y[: tiles - d]], axis=0)
        elif bit < tile_bits + sub_bits:
            d = 1 << (bit - tile_bits)
            y = pltpu.roll(y, d, 1)
            y = jnp.where(iota(dims, 1) < d, pltpu.roll(y, 1, 2), y)
        else:
            y = pltpu.roll(y, 1 << (bit - tile_bits - sub_bits), 2)
        x = jnp.minimum(x, y)
    pos_ref[...] = jnp.where(x < empty, x & ((1 << bits) - 1), -1)


def place_pick(spheres, got_ref, tab_s, pos_ref, terms_ref, col_ref):
    sources, _, cap_rows, _ = got_ref.shape
    groups = range(sources // SUB)
    tiles = K * spheres // TILE

    def pick(q, pos, group, kk, values):
        number = pos >> log2(LANES)
        at = pos & (LANES - 1)
        values = list(values)
        for u in range(SUB):
            s = group * SUB + u
            k = jnp.minimum(tab_s[group, 0, u, q] + kk, cap_rows - 1)
            match = number == s * cap_rows + k
            for c in range(1, SENT):
                row = jnp.broadcast_to(got_ref[s, c, pl.ds(k, 1), :], (SUB, LANES))
                found = jnp.take_along_axis(row, at, axis=1)
                values[c - 1] = jnp.where(match, found, values[c - 1])
        return tuple(values)

    def save(q, values):
        rows = pl.ds(pl.multiple_of(q * SUB, SUB), SUB)
        col_ref[rows, :] = values[0].astype(i32)
        for c in range(SENT - 2):
            terms_ref[c, rows, :] = values[c + 1]

    def first_rows(q, carry):
        pos = pos_ref[q]
        zero = jnp.zeros((SUB, LANES), f32)
        values = (jnp.where(pos >= 0, 0.0, -1.0),) + (zero,) * (SENT - 2)
        for group in groups:
            values = pick(q, pos, group, 0, values)
        save(q, values)
        return carry

    def more_rows(q, carry):
        for group in groups:
            count = tab_s[group, 1, 0, q]

            @pl.when(count > 1)
            def _():
                rows = pl.ds(pl.multiple_of(q * SUB, SUB), SUB)
                pos = pos_ref[q]
                values = (col_ref[rows, :].astype(f32),) + tuple(terms_ref[c, rows, :] for c in range(SENT - 2))
                values = lax.fori_loop(1, count, lambda kk, values: pick(q, pos, group, kk, values), values)
                save(q, values)

        return carry

    lax.fori_loop(0, tiles, first_rows, 0, unroll=4)
    lax.fori_loop(0, tiles, more_rows, 0)


def place_blocks(spheres, col_ref, span_ref):
    lane = iota((SUB, LANES), 1)
    big = float(1 << 20)
    low = jnp.full((SUB, LANES), big, f32)
    high = jnp.full((SUB, LANES), -1.0, f32)
    for q in range(K * spheres // (SUB * LANES)):
        block = (col_ref[q * SUB : (q + 1) * SUB, :] >> log2(spheres)).astype(f32)
        b_low = jnp.min(jnp.where(block < 0.0, big, block), axis=1, keepdims=True)
        b_high = jnp.max(block, axis=1, keepdims=True)
        low = jnp.where(lane == q, b_low, low)
        high = jnp.where(lane == q, b_high, high)
    span_ref[0:SUB, :] = jnp.broadcast_to(jnp.min(low, axis=0, keepdims=True), (SUB, LANES)).astype(i32)
    span_ref[SUB : 2 * SUB, :] = jnp.broadcast_to(jnp.max(high, axis=0, keepdims=True), (SUB, LANES)).astype(i32)


def tile_terms(terms_ref, rows, diff):
    e = [terms_ref[c, rows, :] for c in range(3)]
    c1 = terms_ref[3, rows, :]
    size = e[0] * e[0] + e[1] * e[1] + e[2] * e[2]
    c2 = c1 * (1.0 - size)
    p = e[0] * diff[0] + e[1] * diff[1] + e[2] * diff[2]
    t = e[0] * diff[3] + e[1] * diff[4] + e[2] * diff[5]
    mix = 0.8 * c1
    along_top = 6.0 * c2 * p + mix * t
    along_bottom = mix * p - 2.0 * c1 * t
    cross = mix * (size * (1.0 / 3.0))
    strong = 2.5 * c1
    top = [e[c] * along_top + c1 * diff[c] - cross * diff[3 + c] for c in range(3)]
    return top + [e[c] * along_bottom - cross * diff[c] + strong * diff[3 + c] for c in range(3)]


class Slot:
    def __init__(self, k, halves, span_ref, col_ref):
        self.halves = halves
        self.rows = [pl.ds(pl.multiple_of((k * halves + h) * SUB, SUB), SUB) for h in range(halves)]
        col = [col_ref[r, :] for r in self.rows]
        self.at = [c & (LANES - 1) for c in col]
        self.number = [c >> log2(LANES) for c in col]
        self.low = span_ref[0, k * halves]
        self.high = span_ref[SUB, k * halves]
        for h in range(1, halves):
            self.low = jnp.minimum(self.low, span_ref[0, k * halves + h])
            self.high = jnp.maximum(self.high, span_ref[SUB, k * halves + h])

    def none(self):
        return tuple(jnp.zeros((SUB, LANES), f32) for _ in range(FIELDS * self.halves))

    def gather(self, strip, part, values):
        chunks = part.shape[2]

        def block(b, values):
            values = list(values)
            for r in range(chunks):
                match = [n == b * chunks + r for n in self.number]
                for c in range(FIELDS):
                    row = jnp.broadcast_to(part[b - 3 * strip, c, r : r + 1, :], (SUB, LANES))
                    for h in range(self.halves):
                        found = jnp.take_along_axis(row, self.at[h], axis=1)
                        values[h * FIELDS + c] = jnp.where(match[h], found, values[h * FIELDS + c])
            return tuple(values)

        start = jnp.maximum(self.low, 3 * strip)
        return lax.fori_loop(start, jnp.minimum(self.high, 3 * strip + 2) + 1, block, values)


def apply_inner(mid, span_ref, col_ref, terms_ref, drag_ref, out_ref):
    chunks = mid.shape[2]
    halves = chunks // SUB

    def own(h, c):
        return mid[1, c, h * SUB : (h + 1) * SUB, :]

    def slot(k, sums):
        here = Slot(k, halves, span_ref, col_ref)
        other = here.gather(1, mid, here.none())
        sums = list(sums)
        for h in range(halves):
            diff = [own(h, c) - other[h * FIELDS + c] for c in range(FIELDS)]
            for c, term in enumerate(tile_terms(terms_ref, here.rows[h], diff)):
                sums[h * FIELDS + c] = sums[h * FIELDS + c] + term
        return tuple(sums)

    start = []
    for h in range(halves):
        for c in range(FIELDS):
            start.append(drag_ref[c * chunks + h * SUB : c * chunks + (h + 1) * SUB, :] * own(h, c))
    sums = lax.fori_loop(0, K, slot, tuple(start))
    for h in range(halves):
        for c in range(FIELDS):
            out_ref[c, h * SUB : (h + 1) * SUB, :] = sums[h * FIELDS + c]


def apply_outer(below, above, span_ref, col_ref, terms_ref, part_ref, out_ref):
    halves = below.shape[2] // SUB
    out_ref[...] = part_ref[...]

    def slot(k, carry):
        here = Slot(k, halves, span_ref, col_ref)

        @pl.when(jnp.logical_or(here.low < 3, here.high > 5))
        def _():
            other = here.gather(2, above, here.gather(0, below, here.none()))
            for h in range(halves):
                terms = tile_terms(terms_ref, here.rows[h], other[h * FIELDS : (h + 1) * FIELDS])
                for c, term in enumerate(terms):
                    rows = slice(h * SUB, (h + 1) * SUB)
                    out_ref[c, rows, :] = out_ref[c, rows, :] - term

        return carry

    lax.fori_loop(0, K, slot, 0)


def two_sum(a, b):
    s = a + b
    t = s - a
    return s, (a - (s - t)) + (b - t)


def quick(a, b):
    s = a + b
    return s, b - (s - a)


def halve(a):
    t = a * 4097.0
    high = t - (t - a)
    return high, a - high


def two_prod(a, b, a_parts=None, b_parts=None):
    ah, al = a_parts or halve(a)
    bh, bl = b_parts or halve(b)
    p = a * b
    return p, ((ah * bh - p) + ah * bl + al * bh) + al * bl


class Pair:
    def __init__(self, high, low):
        self.high, self.low = high, low

    def __add__(self, other):
        s, e = two_sum(self.high, other.high)
        return Pair(*quick(s, e + (self.low + other.low)))

    def __neg__(self):
        return Pair(-self.high, -self.low)

    def __mul__(self, other):
        p, e = two_prod(self.high, other.high)
        return Pair(*quick(p, e + (self.high * other.low + self.low * other.high)))

    def __truediv__(self, other):
        q = self.high / other.high
        p, e = two_prod(q, other.high)
        rest = ((self.high - p) - e) + (self.low - q * other.low)
        return Pair(*quick(q, rest / other.high))


GRAM = [(a, b) for a in range(ITERS + 1) for b in range(a, ITERS + 1)]
EARLY = [n for n, (a, b) in enumerate(GRAM) if b < ITERS]
LATE = [n for n, (a, b) in enumerate(GRAM) if b == ITERS]


def gram_row(vectors, wanted):
    zero = jnp.zeros((SUB, LANES), f32)
    sums = [(zero, zero) for _ in wanted]
    fields, chunks, _ = vectors[0].shape
    for c in range(fields):
        for h in range(chunks // SUB):
            x = [v[c, h * SUB : (h + 1) * SUB, :] for v in vectors]
            parts = [halve(a) for a in x]
            for n, (a, b) in enumerate(GRAM[w] for w in wanted):
                p, e = two_prod(x[a], x[b], parts[a], parts[b])
                s, rest = two_sum(sums[n][0], p)
                sums[n] = (s, sums[n][1] + (e + rest))
    lane = iota((SUB, LANES), 1)
    sub = iota((SUB, LANES), 0)
    row = zero
    for base in range(0, len(wanted), SUB):
        packed = (zero, zero)
        spot = zero.astype(i32) - 1
        for n in range(base, min(base + SUB, len(wanted))):
            spot = jnp.where(sub == n - base, wanted[n], spot)
            s, e = sums[n]
            for step in (4, 2, 1):
                s, rest = two_sum(s, pltpu.roll(s, step, 0))
                e = e + pltpu.roll(e, step, 0) + rest
            packed = tuple(jnp.where(sub == n - base, new, old) for new, old in zip((s, e), packed))
        s, e = packed
        for step in (64, 32, 16, 8, 4, 2, 1):
            s, rest = two_sum(s, pltpu.roll(s, step, 1))
            e = e + pltpu.roll(e, step, 1) + rest
        row = row + jnp.where(lane == spot, s, 0.0)
        row = row + jnp.where(jnp.logical_and(spot >= 0, lane == spot + 64), e, 0.0)
    return jnp.sum(row, axis=0, keepdims=True)


def gram_total(rows_ref):
    total = Pair(jnp.zeros((SUB, LANES), f32), jnp.zeros((SUB, LANES), f32))
    for n in range(rows_ref.shape[0] // SUB):
        x = rows_ref[n * SUB : (n + 1) * SUB, :]
        total = total + Pair(x, pltpu.roll(x, 64, 1))
    for step in (4, 2, 1):
        total = total + Pair(pltpu.roll(total.high, step, 0), pltpu.roll(total.low, step, 0))
    grid = {}
    for n, (a, b) in enumerate(GRAM):
        at = jnp.full((SUB, LANES), n, i32)
        grid[a, b] = grid[b, a] = Pair(*quick(*(jnp.take_along_axis(x, at, axis=1) for x in (total.high, total.low))))
    return grid


def weigh(grid, x, y, shift):
    out = None
    for i, a in enumerate(x):
        for j, b in enumerate(y):
            term = grid[i, j + shift] if a is None and b is None else None
            if term is None:
                term = grid[i, j + shift] * (a if b is None else b if a is None else a * b)
            out = term if out is None else out + term
    return out


def conjugate(grid):
    zero = jnp.zeros((SUB, LANES), f32)
    one = Pair(zero + 1.0, zero)
    c = [one]
    d = [one]
    x = []
    norm = grid[0, 0]
    least = None
    for iteration in range(ITERS):
        step = norm / weigh(grid, d, d, 1)
        x = [a + step * b if a is not None else step * b for a, b in zip(x + [None], d)]
        c = [
            (c[n] if n < len(c) else None, -(step * d[n - 1]) if n else None) for n in range(len(d) + 1)
        ]
        c = [a if b is None else b if a is None else a + b for a, b in c]
        new = weigh(grid, c, c, 0)
        least = new.high if least is None else jnp.minimum(least, new.high)
        ratio = new / norm
        d = [a + ratio * b if b is not None else a for a, b in zip(c, d + [None])]
        norm = new
    size = zero
    for n in range(ITERS + 1):
        size = size + jnp.abs(c[n].high) * jnp.sqrt(grid[n, n].high)
    return [a.high for a in x], [a.high for a in c], jnp.where(least > 1e-6 * (size * size), 1.0, 0.0)


def first_kernel(
    spheres, got, drag, below, mid, above, terms, col, span, drag_out, out, part, pos, tab, tab_s, span_s, sem
):
    chunks = spheres // LANES
    place_ranges(got, tab)
    copy = pltpu.make_async_copy(tab, tab_s, sem)
    copy.start()
    for r in range(chunks):
        drag_out[pl.ds(r, FIELDS, stride=chunks), :] = drag[:, r * LANES : (r + 1) * LANES]
    place_sort(got, pos)
    copy.wait()
    place_pick(spheres, got, tab_s, pos, terms, col)
    place_blocks(spheres, col, span)
    copy = pltpu.make_async_copy(span, span_s, sem)
    copy.start()
    copy.wait()
    apply_inner(mid, span_s, col, terms, drag_out, part)
    apply_outer(below, above, span_s, col, terms, part, out)


def inner_kernel(span, col, terms, drag, mid, part):
    apply_inner(mid, span, col, terms, drag, part)


def outer_kernel(span, col, terms, part, below, above, out):
    apply_outer(below, above, span, col, terms, part, out)


def inner_gram_kernel(span, col, terms, drag, mid, k0, k1, part, row):
    apply_inner(mid, span, col, terms, drag, part)
    row[...] = jnp.broadcast_to(gram_row([k0, k1, mid.at[1]], EARLY), row.shape)


def outer_gram_kernel(span, col, terms, part, below, above, k0, k1, k2, row, out, rows):
    apply_outer(below, above, span, col, terms, part, out)
    late = row[0:1, :] + gram_row([k0, k1, k2, out], LATE)
    rows[...] = jnp.broadcast_to(late, rows.shape)


def last_kernel(rows, k0, k1, k2, k3, velocity, residual, good, dense, flat, sem):
    x, c, ok = conjugate(gram_total(rows))
    chunks = k0.shape[1]
    k = [k0, k1, k2, k3]
    for n in range(k0.shape[0]):
        for h in range(chunks // SUB):
            part = [a[n, h * SUB : (h + 1) * SUB, :] for a in k]
            here = slice(n * chunks + h * SUB, n * chunks + (h + 1) * SUB)
            dense[0, here, :] = x[0] * part[0] + x[1] * part[1] + x[2] * part[2]
            dense[1, here, :] = part[0] + c[1] * part[1] + c[2] * part[2] + c[3] * part[3]
    copies = []
    for out, target in enumerate((velocity, residual)):
        for r in range(chunks):
            flat[out, :, r * LANES : (r + 1) * LANES] = dense[out, pl.ds(r, FIELDS, stride=chunks), :]
        copies.append(pltpu.make_async_copy(flat.at[out], target, sem.at[out]))
        copies[-1].start()
    good[0, 0] = jnp.min(ok).astype(i32)
    for copy in copies:
        copy.wait()


VMEM = pl.BlockSpec(memory_space=pltpu.VMEM)
SMEM = pl.BlockSpec(memory_space=pltpu.SMEM)
HBM = pl.BlockSpec(memory_space=pltpu.HBM)
PARAMS = pltpu.CompilerParams(vmem_limit_bytes=24 << 20)


def shape(dims, dtype=f32):
    return jax.ShapeDtypeStruct(dims, dtype)


def ring(axis, step):
    count = lax.axis_size(axis)
    return [(i, (i + step) % count) for i in range(count)]


def beside(x):
    west = lax.ppermute(x, "gx", ring("gx", 1))
    east = lax.ppermute(x, "gx", ring("gx", -1))
    mid = jnp.stack([west, x, east])
    below = lax.ppermute(mid, "gy", ring("gy", 1))
    above = lax.ppermute(mid, "gy", ring("gy", -1))
    return below, mid, above


def plain(apply, forces):
    def both(a, b):
        return lax.psum(jnp.sum(a * b), ("gx", "gy"))

    velocity = jnp.zeros_like(forces)
    residual = direction = forces
    norm = both(residual, residual)
    for iteration in range(ITERS):
        applied = apply(direction)
        step = norm / both(direction, applied)
        velocity = velocity + step * direction
        residual = residual - step * applied
        new = both(residual, residual)
        direction = residual + new / norm * direction
        norm = new
    return velocity, residual


def on_device(pair_ends, pair_geometry, drag_coef, forces):
    spheres = drag_coef.shape[1]
    chunks = spheres // LANES
    slabs = lax.axis_size("gx")
    devices = slabs * lax.axis_size("gy")
    field = (FIELDS, chunks, LANES)
    slot_rows = K * spheres // LANES
    dense = pltpu.VMEM(field, f32)
    ranges = (slabs // SUB, 2, SUB, LANES)
    assert K * spheres == SUB * 4 * TILE and slabs % SUB == 0
    send, k0 = pack(pair_ends, pair_geometry, forces, slabs, lax.axis_size("gy"))
    got = lax.all_to_all(send, "gx", split_axis=0, concat_axis=0, tiled=True)
    k0 = k0.reshape(field)
    terms, col, span, drag, k1 = pl.pallas_call(
        functools.partial(first_kernel, spheres),
        out_shape=(
            shape((SENT - 2, slot_rows, LANES)),
            shape((slot_rows, LANES), i32),
            shape((2 * SUB, LANES), i32),
            shape((FIELDS * chunks, LANES)),
            shape(field),
        ),
        in_specs=[VMEM] * 5,
        scratch_shapes=[
            dense,
            pltpu.VMEM((slot_rows // SUB, SUB, LANES), i32),
            pltpu.VMEM(ranges, i32),
            pltpu.SMEM(ranges, i32),
            pltpu.SMEM((2 * SUB, LANES), i32),
            pltpu.SemaphoreType.DMA,
        ],
        compiler_params=PARAMS,
        name="first",
    )(got, drag_coef, *beside(k0))

    def local(kernel, name, outs, cost, *args):
        return pl.pallas_call(
            kernel,
            out_shape=outs,
            in_specs=[SMEM] + [VMEM] * (len(args) + 2),
            compiler_params=PARAMS,
            cost_estimate=pl.CostEstimate(flops=0, bytes_accessed=cost << 20, transcendentals=0),
            name=name,
        )(span, col, terms, *args)

    def apply(x):
        below, mid, above = beside(x)
        part = local(inner_kernel, "inner", shape(field), 16, drag, mid)
        return local(outer_kernel, "outer", shape(field), 16, part, below, above)

    k2 = apply(k1)
    below, mid, above = beside(k2)
    part, row = local(
        inner_gram_kernel, "inner_gram", (shape(field), shape((SUB, LANES))), 16, drag, mid, k0, k1
    )
    k3, rows = local(
        outer_gram_kernel, "outer_gram", (shape(field), shape((devices, LANES))), 16,
        part, below, above, k0, k1, k2, row,
    )
    rows = lax.all_to_all(rows, ("gx", "gy"), split_axis=0, concat_axis=0, tiled=True)
    velocity, residual, good = pl.pallas_call(
        last_kernel,
        out_shape=(shape((FIELDS, spheres)), shape((FIELDS, spheres)), shape((1, 1), i32)),
        out_specs=(HBM, HBM, SMEM),
        scratch_shapes=[
            pltpu.VMEM((2, FIELDS * chunks, LANES), f32),
            pltpu.VMEM((2, FIELDS, spheres), f32),
            pltpu.SemaphoreType.DMA((2,)),
        ],
        compiler_params=PARAMS,
        name="last",
    )(rows, k0, k1, k2, k3)

    def again(state):
        v, r = plain(apply, k0)
        return jnp.ones_like(good), v.reshape(FIELDS, spheres), r.reshape(FIELDS, spheres)

    return lax.while_loop(lambda state: state[0][0, 0] == 0, again, (good, velocity, residual))[1:]


def solution(mesh):
    spec = P(None, ("gx", "gy"))
    return jax.shard_map(
        on_device, mesh=mesh, in_specs=(spec,) * 4, out_specs=(spec, spec), check_vma=False
    )
```

```python
import functools

import jax
import jax.numpy as jnp
from jax import lax
from jax.experimental import pallas as pl
from jax.experimental.pallas import tpu as pltpu
from jax.sharding import PartitionSpec as P

K = 16
ITERS = 3
LANES = 128
SUB = 8
FIELDS = 6
SENT = 6
TILE = SUB * LANES

f32 = jnp.float32
i32 = jnp.int32
bf16 = jnp.bfloat16


def log2(n):
    assert n & (n - 1) == 0
    return n.bit_length() - 1


def iota(shape, dim):
    return lax.broadcasted_iota(i32, shape, dim)


def pack_kernel(slabs, strips, spheres, ends_ref, geo_ref, force_ref, send_ref, dense_ref, ends_s, geo_s, out_s):
    rows = ends_ref.shape[1] // LANES
    padded = ends_s.shape[0] // 3
    cap_rows = send_ref.shape[2]
    chunks = spheres // LANES
    for r in range(rows):
        cols = slice(r * LANES, (r + 1) * LANES)
        ends_s[pl.ds(r, 3, stride=padded), :] = ends_ref[:, cols]
        geo_s[pl.ds(r, 5, stride=padded), :] = geo_ref[:, cols]
    for r in range(chunks):
        dense_ref[pl.ds(r, FIELDS, stride=chunks), :] = force_ref[:, r * LANES : (r + 1) * LANES]
    first = ends_s[0:padded, :]
    second = ends_s[padded : 2 * padded, :]
    slot = ends_s[2 * padded : 3 * padded, :]
    inside = iota((padded, LANES), 0) < rows
    live = jnp.logical_and(slot < K, inside)
    shift = log2(spheres)
    first_block = first >> shift
    second_block = second >> shift
    owner = first_block >> log2(strips)
    shift_x = ((second_block >> log2(strips)) - owner + 1) & (slabs - 1)
    apart = (second_block ^ first_block) & (strips - 1)
    strip = jnp.where(apart == 0, 0, jnp.where(apart == 1, 1, 2))
    column = (strip * 3 + shift_x) * spheres + (second & (spheres - 1))
    place = first & (spheres - 1)
    tile = slot * (spheres // TILE) + (place >> log2(TILE))
    target = ((place & (LANES - 1)) * SUB + ((place >> log2(LANES)) & (SUB - 1))) * (K * spheres // TILE) + tile
    owner = jnp.where(live, owner, slabs)
    sep = [geo_s[c * padded : (c + 1) * padded, :] for c in range(3)]
    a = geo_s[3 * padded : 4 * padded, :]
    b = geo_s[4 * padded : 5 * padded, :]
    h = a + b
    total = sep[0] * sep[0] + sep[1] * sep[1] + sep[2] * sep[2] + h * h
    inv = lax.rsqrt(total)
    values = [target.astype(f32), column.astype(f32)] + [d * inv for d in sep] + [a * b * h * (inv * inv)]
    for c, value in enumerate(values):
        out_s[c, 0:padded, :] = value
    lane = iota((cap_rows, LANES), 1)
    place = iota((cap_rows, LANES), 0) * LANES + lane
    ends = [jnp.sum(jnp.where(owner <= o, 1.0, 0.0)).astype(i32) for o in range(slabs)]
    start = jnp.int32(0)
    for o in range(slabs):
        end = ends[o]
        row = start >> 7
        off = start & (LANES - 1)
        back = (LANES - off) & (LANES - 1)
        for c in range(SENT):
            here = pltpu.roll(out_s[c, pl.ds(row, cap_rows), :], back, 1)
            after = pltpu.roll(out_s[c, pl.ds(row + 1, cap_rows), :], back, 1)
            value = jnp.where(lane < LANES - off, here, after)
            if c == 0:
                value = jnp.where(place < end - start, value, -1.0)
            send_ref[o, c] = value
        start = end


def pack(ends, geo, forces, slabs, strips):
    spheres = forces.shape[1]
    cap_rows = spheres * K // slabs // LANES
    rows = ends.shape[1] // LANES
    padded = -(-rows // SUB) * SUB
    return pl.pallas_call(
        functools.partial(pack_kernel, slabs, strips, spheres),
        out_shape=(
            jax.ShapeDtypeStruct((slabs, SENT, cap_rows, LANES), f32),
            jax.ShapeDtypeStruct((FIELDS * spheres // LANES, LANES), f32),
        ),
        scratch_shapes=[
            pltpu.VMEM((3 * padded, LANES), i32),
            pltpu.VMEM((5 * padded, LANES), f32),
            pltpu.VMEM((SENT, padded + cap_rows + SUB, LANES), f32),
        ],
        name="pack",
    )(ends, geo, forces)


def place_ranges(got_ref, tab_v):
    sources, _, cap_rows, _ = got_ref.shape
    tiles = sources * cap_rows // SUB
    lane = iota((SUB, LANES), 1)
    lane_f = lane.astype(f32)
    big = float(1 << 20)
    for group in range(sources // SUB):
        low = jnp.full((SUB, LANES), big, f32)
        high = jnp.full((SUB, LANES), -1.0, f32)
        for k in range(cap_rows):
            t = got_ref[group * SUB : (group + 1) * SUB, 0, k, :]
            tile = t - float(tiles) * jnp.floor(t * (1.0 / tiles))
            t_low = jnp.min(jnp.where(t < 0.0, big, tile), axis=1, keepdims=True)
            t_high = jnp.max(jnp.where(t < 0.0, -1.0, tile), axis=1, keepdims=True)
            low = jnp.where(lane == k, t_low, low)
            high = jnp.where(lane == k, t_high, high)
        starts = jnp.zeros((SUB, LANES), f32)
        counts = jnp.zeros((SUB, LANES), f32)
        for q in range(tiles):
            hit = jnp.logical_and(low <= q, high >= q)
            k_low = jnp.min(jnp.where(hit, lane_f, float(cap_rows - 1)), axis=1, keepdims=True)
            k_high = jnp.max(jnp.where(hit, lane_f, -1.0), axis=1, keepdims=True)
            starts = jnp.where(lane == q, k_low, starts)
            counts = jnp.where(lane == q, k_high - k_low + 1.0, counts)
        tab_v[group, 0] = starts.astype(i32)
        tab_v[group, 1] = jnp.broadcast_to(jnp.max(counts, axis=0, keepdims=True), (SUB, LANES)).astype(i32)


def place_sort(got_ref, pos_ref):
    sources, _, cap_rows, _ = got_ref.shape
    tiles = sources * cap_rows // SUB
    dims = (tiles, SUB, LANES)
    tile_bits, sub_bits = log2(tiles), log2(SUB)
    bits = log2(tiles * TILE)
    empty = 1 << (2 * bits)
    t = got_ref[:, 0].reshape(dims).astype(i32)
    home = (iota(dims, 0) * SUB + iota(dims, 1)) * LANES + iota(dims, 2)
    x = jnp.where(t < 0, empty, t << bits) + home
    place = (iota(dims, 2) * SUB + iota(dims, 1)) * tiles + iota(dims, 0)

    def partner(x, bit):
        axis, size, d = (1, SUB, 1 << (bit - tile_bits)) if bit < tile_bits + sub_bits else (
            2, LANES, 1 << (bit - tile_bits - sub_bits))
        if 2 * d == size:
            return pltpu.roll(x, d, axis)
        upper = (iota(dims, axis) & d) != 0
        return jnp.where(upper, pltpu.roll(x, d, axis), pltpu.roll(x, size - d, axis))

    def exchange(x, bit):
        if bit < tile_bits:
            pairs = x.reshape((tiles >> (bit + 1), 2, 1 << bit, SUB, LANES))
            low = jnp.minimum(pairs[:, 0:1], pairs[:, 1:2])
            high = jnp.maximum(pairs[:, 0:1], pairs[:, 1:2])
            return jnp.concatenate([low, high], axis=1).reshape(dims)
        other = partner(x, bit)
        upper = (place & (1 << bit)) != 0
        return jnp.where(jnp.logical_xor(x < other, upper), x, other)

    for m in range(1, bits + 1):
        flip = -(((place >> m) ^ (place >> (m - 1) if m > 1 else 0)) & 1)
        x = x ^ flip
        for bit in range(m - 1, -1, -1):
            x = exchange(x, bit)

    def carry(x):
        x = pltpu.roll(x, 1, 1)
        return jnp.where(iota(x.shape, 1) < 1, pltpu.roll(x, 1, 2), x)

    for bit in range(bits - 1, -1, -1):
        move = jnp.logical_and(x < empty, x - (place << bits) >= (1 << (bit + bits)))
        y = jnp.where(move, x, empty)
        x = jnp.where(move, empty, x)
        if bit < tile_bits:
            d = 1 << bit
            y = jnp.concatenate([carry(y[tiles - d :]), y[: tiles - d]], axis=0)
        elif bit < tile_bits + sub_bits:
            d = 1 << (bit - tile_bits)
            y = pltpu.roll(y, d, 1)
            y = jnp.where(iota(dims, 1) < d, pltpu.roll(y, 1, 2), y)
        else:
            y = pltpu.roll(y, 1 << (bit - tile_bits - sub_bits), 2)
        x = jnp.minimum(x, y)
    pos_ref[...] = jnp.where(x < empty, x & ((1 << bits) - 1), -1)


def place_pick(spheres, got_ref, tab_s, pos_ref, terms_ref, col_ref):
    sources, _, cap_rows, _ = got_ref.shape
    groups = range(sources // SUB)
    tiles = K * spheres // TILE

    def pick(q, pos, group, kk, values):
        number = pos >> log2(LANES)
        at = pos & (LANES - 1)
        values = list(values)
        for u in range(SUB):
            s = group * SUB + u
            k = jnp.minimum(tab_s[group, 0, u, q] + kk, cap_rows - 1)
            match = number == s * cap_rows + k
            for c in range(1, SENT):
                row = jnp.broadcast_to(got_ref[s, c, pl.ds(k, 1), :], (SUB, LANES))
                found = jnp.take_along_axis(row, at, axis=1)
                values[c - 1] = jnp.where(match, found, values[c - 1])
        return tuple(values)

    def save(q, values):
        rows = pl.ds(pl.multiple_of(q * SUB, SUB), SUB)
        col_ref[rows, :] = values[0].astype(i32)
        for c in range(SENT - 2):
            terms_ref[c, rows, :] = values[c + 1]

    def first_rows(q, carry):
        pos = pos_ref[q]
        zero = jnp.zeros((SUB, LANES), f32)
        values = (jnp.where(pos >= 0, 0.0, -1.0),) + (zero,) * (SENT - 2)
        for group in groups:
            values = pick(q, pos, group, 0, values)
        save(q, values)
        return carry

    def more_rows(q, carry):
        for group in groups:
            count = tab_s[group, 1, 0, q]

            @pl.when(count > 1)
            def _():
                rows = pl.ds(pl.multiple_of(q * SUB, SUB), SUB)
                pos = pos_ref[q]
                values = (col_ref[rows, :].astype(f32),) + tuple(terms_ref[c, rows, :] for c in range(SENT - 2))
                values = lax.fori_loop(1, count, lambda kk, values: pick(q, pos, group, kk, values), values)
                save(q, values)

        return carry

    lax.fori_loop(0, tiles, first_rows, 0, unroll=4)
    lax.fori_loop(0, tiles, more_rows, 0)


def place_blocks(spheres, col_ref, span_ref):
    lane = iota((SUB, LANES), 1)
    big = float(1 << 20)
    low = jnp.full((SUB, LANES), big, f32)
    high = jnp.full((SUB, LANES), -1.0, f32)
    for q in range(K * spheres // (SUB * LANES)):
        block = (col_ref[q * SUB : (q + 1) * SUB, :] >> log2(spheres)).astype(f32)
        b_low = jnp.min(jnp.where(block < 0.0, big, block), axis=1, keepdims=True)
        b_high = jnp.max(block, axis=1, keepdims=True)
        low = jnp.where(lane == q, b_low, low)
        high = jnp.where(lane == q, b_high, high)
    span_ref[0:SUB, :] = jnp.broadcast_to(jnp.min(low, axis=0, keepdims=True), (SUB, LANES)).astype(i32)
    span_ref[SUB : 2 * SUB, :] = jnp.broadcast_to(jnp.max(high, axis=0, keepdims=True), (SUB, LANES)).astype(i32)


def tile_terms(terms_ref, rows, diff):
    e = [terms_ref[c, rows, :] for c in range(3)]
    c1 = terms_ref[3, rows, :]
    size = e[0] * e[0] + e[1] * e[1] + e[2] * e[2]
    c2 = c1 * (1.0 - size)
    p = e[0] * diff[0] + e[1] * diff[1] + e[2] * diff[2]
    t = e[0] * diff[3] + e[1] * diff[4] + e[2] * diff[5]
    mix = 0.8 * c1
    along_top = 6.0 * c2 * p + mix * t
    along_bottom = mix * p - 2.0 * c1 * t
    cross = mix * (size * (1.0 / 3.0))
    strong = 2.5 * c1
    top = [e[c] * along_top + c1 * diff[c] - cross * diff[3 + c] for c in range(3)]
    return top + [e[c] * along_bottom - cross * diff[c] + strong * diff[3 + c] for c in range(3)]


class Slot:
    def __init__(self, k, halves, span_ref, col_ref):
        self.halves = halves
        self.rows = [pl.ds(pl.multiple_of((k * halves + h) * SUB, SUB), SUB) for h in range(halves)]
        col = [col_ref[r, :] for r in self.rows]
        self.at = [c & (LANES - 1) for c in col]
        self.number = [c >> log2(LANES) for c in col]
        self.low = span_ref[0, k * halves]
        self.high = span_ref[SUB, k * halves]
        for h in range(1, halves):
            self.low = jnp.minimum(self.low, span_ref[0, k * halves + h])
            self.high = jnp.maximum(self.high, span_ref[SUB, k * halves + h])

    def none(self):
        return tuple(jnp.zeros((SUB, LANES), f32) for _ in range(FIELDS * self.halves))

    def gather(self, strip, part, values):
        chunks = part.shape[2]

        def block(b, values):
            values = list(values)
            for r in range(chunks):
                match = [n == b * chunks + r for n in self.number]
                for c in range(FIELDS):
                    row = jnp.broadcast_to(part[b - 3 * strip, c, r : r + 1, :], (SUB, LANES))
                    for h in range(self.halves):
                        found = jnp.take_along_axis(row, self.at[h], axis=1)
                        values[h * FIELDS + c] = jnp.where(match[h], found, values[h * FIELDS + c])
            return tuple(values)

        start = jnp.maximum(self.low, 3 * strip)
        return lax.fori_loop(start, jnp.minimum(self.high, 3 * strip + 2) + 1, block, values)


def apply_inner(mid, near, span_ref, col_ref, terms_ref, drag_ref, out_ref):
    chunks = mid.shape[2]
    halves = chunks // SUB

    def own(h, c):
        return mid[1, c, h * SUB : (h + 1) * SUB, :]

    def slot(k, sums):
        here = Slot(k, halves, span_ref, col_ref)
        other = here.gather(1, near, here.gather(0, mid, here.none()))
        sums = list(sums)
        for h in range(halves):
            diff = [own(h, c) - other[h * FIELDS + c] for c in range(FIELDS)]
            for c, term in enumerate(tile_terms(terms_ref, here.rows[h], diff)):
                sums[h * FIELDS + c] = sums[h * FIELDS + c] + term
        return tuple(sums)

    start = []
    for h in range(halves):
        for c in range(FIELDS):
            start.append(drag_ref[c * chunks + h * SUB : c * chunks + (h + 1) * SUB, :] * own(h, c))
    sums = lax.fori_loop(0, K, slot, tuple(start))
    for h in range(halves):
        for c in range(FIELDS):
            out_ref[c, h * SUB : (h + 1) * SUB, :] = sums[h * FIELDS + c]


def apply_outer(far, span_ref, col_ref, terms_ref, part_ref, out_ref):
    halves = far.shape[2] // SUB
    out_ref[...] = part_ref[...]

    def slot(k, carry):
        here = Slot(k, halves, span_ref, col_ref)

        @pl.when(here.high >= 6)
        def _():
            other = here.gather(2, far, here.none())
            for h in range(halves):
                terms = tile_terms(terms_ref, here.rows[h], other[h * FIELDS : (h + 1) * FIELDS])
                for c, term in enumerate(terms):
                    rows = slice(h * SUB, (h + 1) * SUB)
                    out_ref[c, rows, :] = out_ref[c, rows, :] - term

        return carry

    lax.fori_loop(0, K, slot, 0)


def two_sum(a, b):
    s = a + b
    t = s - a
    return s, (a - (s - t)) + (b - t)


def quick(a, b):
    s = a + b
    return s, b - (s - a)


def halve(a):
    t = a * 4097.0
    high = t - (t - a)
    return high, a - high


def two_prod(a, b, a_parts=None, b_parts=None):
    ah, al = a_parts or halve(a)
    bh, bl = b_parts or halve(b)
    p = a * b
    return p, ((ah * bh - p) + ah * bl + al * bh) + al * bl


class Pair:
    def __init__(self, high, low):
        self.high, self.low = high, low

    def __add__(self, other):
        s, e = two_sum(self.high, other.high)
        return Pair(*quick(s, e + (self.low + other.low)))

    def __neg__(self):
        return Pair(-self.high, -self.low)

    def __mul__(self, other):
        p, e = two_prod(self.high, other.high)
        return Pair(*quick(p, e + (self.high * other.low + self.low * other.high)))

    def __truediv__(self, other):
        q = self.high / other.high
        p, e = two_prod(q, other.high)
        rest = ((self.high - p) - e) + (self.low - q * other.low)
        return Pair(*quick(q, rest / other.high))


GRAM = [(a, b) for a in range(ITERS + 1) for b in range(a, ITERS + 1)]
EARLY = [n for n, (a, b) in enumerate(GRAM) if b < ITERS]
LATE = [n for n, (a, b) in enumerate(GRAM) if b == ITERS]


def gram_row(vectors, wanted):
    zero = jnp.zeros((SUB, LANES), f32)
    sums = [(zero, zero) for _ in wanted]
    fields, chunks, _ = vectors[0].shape
    for c in range(fields):
        for h in range(chunks // SUB):
            x = [v[c, h * SUB : (h + 1) * SUB, :] for v in vectors]
            parts = [halve(a) for a in x]
            for n, (a, b) in enumerate(GRAM[w] for w in wanted):
                p, e = two_prod(x[a], x[b], parts[a], parts[b])
                s, rest = two_sum(sums[n][0], p)
                sums[n] = (s, sums[n][1] + (e + rest))
    lane = iota((SUB, LANES), 1)
    sub = iota((SUB, LANES), 0)
    row = zero
    for base in range(0, len(wanted), SUB):
        packed = (zero, zero)
        spot = zero.astype(i32) - 1
        for n in range(base, min(base + SUB, len(wanted))):
            spot = jnp.where(sub == n - base, wanted[n], spot)
            s, e = sums[n]
            for step in (4, 2, 1):
                s, rest = two_sum(s, pltpu.roll(s, step, 0))
                e = e + pltpu.roll(e, step, 0) + rest
            packed = tuple(jnp.where(sub == n - base, new, old) for new, old in zip((s, e), packed))
        s, e = packed
        for step in (64, 32, 16, 8, 4, 2, 1):
            s, rest = two_sum(s, pltpu.roll(s, step, 1))
            e = e + pltpu.roll(e, step, 1) + rest
        row = row + jnp.where(lane == spot, s, 0.0)
        row = row + jnp.where(jnp.logical_and(spot >= 0, lane == spot + 64), e, 0.0)
    return jnp.sum(row, axis=0, keepdims=True)


def gram_total(rows_ref):
    total = Pair(jnp.zeros((SUB, LANES), f32), jnp.zeros((SUB, LANES), f32))
    for n in range(rows_ref.shape[0] // SUB):
        x = rows_ref[n * SUB : (n + 1) * SUB, :]
        total = total + Pair(x, pltpu.roll(x, 64, 1))
    for step in (4, 2, 1):
        total = total + Pair(pltpu.roll(total.high, step, 0), pltpu.roll(total.low, step, 0))
    grid = {}
    for n, (a, b) in enumerate(GRAM):
        at = jnp.full((SUB, LANES), n, i32)
        grid[a, b] = grid[b, a] = Pair(*quick(*(jnp.take_along_axis(x, at, axis=1) for x in (total.high, total.low))))
    return grid


def weigh(grid, x, y, shift):
    out = None
    for i, a in enumerate(x):
        for j, b in enumerate(y):
            term = grid[i, j + shift] if a is None and b is None else None
            if term is None:
                term = grid[i, j + shift] * (a if b is None else b if a is None else a * b)
            out = term if out is None else out + term
    return out


def conjugate(grid):
    zero = jnp.zeros((SUB, LANES), f32)
    one = Pair(zero + 1.0, zero)
    c = [one]
    d = [one]
    x = []
    norm = grid[0, 0]
    least = None
    for iteration in range(ITERS):
        step = norm / weigh(grid, d, d, 1)
        x = [a + step * b if a is not None else step * b for a, b in zip(x + [None], d)]
        c = [
            (c[n] if n < len(c) else None, -(step * d[n - 1]) if n else None) for n in range(len(d) + 1)
        ]
        c = [a if b is None else b if a is None else a + b for a, b in c]
        new = weigh(grid, c, c, 0)
        least = new.high if least is None else jnp.minimum(least, new.high)
        ratio = new / norm
        d = [a + ratio * b if b is not None else a for a, b in zip(c, d + [None])]
        norm = new
    size = zero
    for n in range(ITERS + 1):
        size = size + jnp.abs(c[n].high) * jnp.sqrt(grid[n, n].high)
    return [a.high for a in x], [a.high for a in c], jnp.where(least > 1e-6 * (size * size), 1.0, 0.0)


def first_kernel(
    spheres, got, drag, mid, near, terms, col, span, drag_out, part, pos, tab, tab_s, span_s, sem
):
    chunks = spheres // LANES
    place_ranges(got, tab)
    copy = pltpu.make_async_copy(tab, tab_s, sem)
    copy.start()
    for r in range(chunks):
        drag_out[pl.ds(r, FIELDS, stride=chunks), :] = drag[:, r * LANES : (r + 1) * LANES]
    place_sort(got, pos)
    copy.wait()
    place_pick(spheres, got, tab_s, pos, terms, col)
    place_blocks(spheres, col, span)
    copy = pltpu.make_async_copy(span, span_s, sem)
    copy.start()
    copy.wait()
    apply_inner(mid, near, span_s, col, terms, drag_out, part)


def inner_kernel(span, col, terms, drag, mid, near, part):
    apply_inner(mid, near, span, col, terms, drag, part)


def outer_kernel(span, col, terms, part, far, out):
    apply_outer(far, span, col, terms, part, out)


def inner_gram_kernel(span, col, terms, drag, mid, near, k0, k1, part, row):
    apply_inner(mid, near, span, col, terms, drag, part)
    row[...] = jnp.broadcast_to(gram_row([k0, k1, mid.at[1]], EARLY), row.shape)


def outer_gram_kernel(span, col, terms, part, far, k0, k1, k2, row, out, rows):
    apply_outer(far, span, col, terms, part, out)
    late = row[0:1, :] + gram_row([k0, k1, k2, out], LATE)
    rows[...] = jnp.broadcast_to(late, rows.shape)


def last_kernel(rows, k0, k1, k2, k3, velocity, residual, good, dense, flat, sem):
    x, c, ok = conjugate(gram_total(rows))
    chunks = k0.shape[1]
    k = [k0, k1, k2, k3]
    for n in range(k0.shape[0]):
        for h in range(chunks // SUB):
            part = [a[n, h * SUB : (h + 1) * SUB, :] for a in k]
            here = slice(n * chunks + h * SUB, n * chunks + (h + 1) * SUB)
            dense[0, here, :] = x[0] * part[0] + x[1] * part[1] + x[2] * part[2]
            dense[1, here, :] = part[0] + c[1] * part[1] + c[2] * part[2] + c[3] * part[3]
    copies = []
    for out, target in enumerate((velocity, residual)):
        for r in range(chunks):
            flat[out, :, r * LANES : (r + 1) * LANES] = dense[out, pl.ds(r, FIELDS, stride=chunks), :]
        copies.append(pltpu.make_async_copy(flat.at[out], target, sem.at[out]))
        copies[-1].start()
    good[0, 0] = jnp.min(ok).astype(i32)
    for copy in copies:
        copy.wait()


VMEM = pl.BlockSpec(memory_space=pltpu.VMEM)
SMEM = pl.BlockSpec(memory_space=pltpu.SMEM)
HBM = pl.BlockSpec(memory_space=pltpu.HBM)
PARAMS = pltpu.CompilerParams(vmem_limit_bytes=24 << 20)


def shape(dims, dtype=f32):
    return jax.ShapeDtypeStruct(dims, dtype)


def ring(axis, step):
    count = lax.axis_size(axis)
    return [(i, (i + step) % count) for i in range(count)]


def beside(x):
    west = lax.ppermute(x, "gx", ring("gx", 1))
    east = lax.ppermute(x, "gx", ring("gx", -1))
    mid = jnp.stack([west, x, east])
    count = lax.axis_size("gy")
    near = lax.ppermute(mid, "gy", [(i, i ^ 1) for i in range(count)])
    far = lax.ppermute(mid, "gy", [(i, (i + 1 if i % 2 else i - 1) % count) for i in range(count)])
    return mid, near, far


def plain(apply, forces):
    def both(a, b):
        return lax.psum(jnp.sum(a * b), ("gx", "gy"))

    velocity = jnp.zeros_like(forces)
    residual = direction = forces
    norm = both(residual, residual)
    for iteration in range(ITERS):
        applied = apply(direction)
        step = norm / both(direction, applied)
        velocity = velocity + step * direction
        residual = residual - step * applied
        new = both(residual, residual)
        direction = residual + new / norm * direction
        norm = new
    return velocity, residual


def on_device(pair_ends, pair_geometry, drag_coef, forces):
    spheres = drag_coef.shape[1]
    chunks = spheres // LANES
    slabs = lax.axis_size("gx")
    devices = slabs * lax.axis_size("gy")
    field = (FIELDS, chunks, LANES)
    slot_rows = K * spheres // LANES
    ranges = (slabs // SUB, 2, SUB, LANES)
    assert K * spheres == SUB * 4 * TILE and slabs % SUB == 0
    send, k0 = pack(pair_ends, pair_geometry, forces, slabs, lax.axis_size("gy"))
    got = lax.all_to_all(send, "gx", split_axis=0, concat_axis=0, tiled=True)
    k0 = k0.reshape(field)
    mid, near, far = beside(k0)
    terms, col, span, drag, part = pl.pallas_call(
        functools.partial(first_kernel, spheres),
        out_shape=(
            shape((SENT - 2, slot_rows, LANES)),
            shape((slot_rows, LANES), i32),
            shape((2 * SUB, LANES), i32),
            shape((FIELDS * chunks, LANES)),
            shape(field),
        ),
        in_specs=[VMEM] * 4,
        scratch_shapes=[
            pltpu.VMEM((slot_rows // SUB, SUB, LANES), i32),
            pltpu.VMEM(ranges, i32),
            pltpu.SMEM(ranges, i32),
            pltpu.SMEM((2 * SUB, LANES), i32),
            pltpu.SemaphoreType.DMA,
        ],
        compiler_params=PARAMS,
        cost_estimate=pl.CostEstimate(flops=0, bytes_accessed=48 << 20, transcendentals=0),
        name="first",
    )(got, drag_coef, mid, near)

    def local(kernel, name, outs, cost, *args):
        return pl.pallas_call(
            kernel,
            out_shape=outs,
            in_specs=[SMEM] + [VMEM] * (len(args) + 2),
            compiler_params=PARAMS,
            cost_estimate=pl.CostEstimate(flops=0, bytes_accessed=cost << 20, transcendentals=0),
            name=name,
        )(span, col, terms, *args)

    k1 = local(outer_kernel, "outer", shape(field), 16, part, far)

    def apply(x):
        mid, near, far = beside(x)
        part = local(inner_kernel, "inner", shape(field), 16, drag, mid, near)
        return local(outer_kernel, "outer", shape(field), 16, part, far)

    k2 = apply(k1)
    mid, near, far = beside(k2)
    part, row = local(
        inner_gram_kernel, "inner_gram", (shape(field), shape((SUB, LANES))), 16, drag, mid, near, k0, k1
    )
    k3, rows = local(
        outer_gram_kernel, "outer_gram", (shape(field), shape((devices, LANES))), 16, part, far, k0, k1, k2, row
    )
    rows = lax.all_to_all(rows, ("gx", "gy"), split_axis=0, concat_axis=0, tiled=True)
    velocity, residual, good = pl.pallas_call(
        last_kernel,
        out_shape=(shape((FIELDS, spheres)), shape((FIELDS, spheres)), shape((1, 1), i32)),
        out_specs=(HBM, HBM, SMEM),
        scratch_shapes=[
            pltpu.VMEM((2, FIELDS * chunks, LANES), f32),
            pltpu.VMEM((2, FIELDS, spheres), f32),
            pltpu.SemaphoreType.DMA((2,)),
        ],
        compiler_params=PARAMS,
        name="last",
    )(rows, k0, k1, k2, k3)

    def again(state):
        v, r = plain(apply, k0)
        return jnp.ones_like(good), v.reshape(FIELDS, spheres), r.reshape(FIELDS, spheres)

    return lax.while_loop(lambda state: state[0][0, 0] == 0, again, (good, velocity, residual))[1:]


def solution(mesh):
    spec = P(None, ("gx", "gy"))
    return jax.shard_map(
        on_device, mesh=mesh, in_specs=(spec,) * 4, out_specs=(spec, spec), check_vma=False
    )
```

```python
import functools

import jax
import jax.numpy as jnp
from jax import lax
from jax.experimental import pallas as pl
from jax.experimental.pallas import tpu as pltpu
from jax.sharding import PartitionSpec as P

K = 16
ITERS = 3
LANES = 128
SUB = 8
FIELDS = 6
SENT = 6
TILE = SUB * LANES

f32 = jnp.float32
i32 = jnp.int32
bf16 = jnp.bfloat16


def log2(n):
    assert n & (n - 1) == 0
    return n.bit_length() - 1


def iota(shape, dim):
    return lax.broadcasted_iota(i32, shape, dim)


def pack_kernel(slabs, strips, spheres, ends_ref, geo_ref, force_ref, send_ref, dense_ref, ends_s, geo_s, out_s):
    rows = ends_ref.shape[1] // LANES
    padded = ends_s.shape[0] // 3
    cap_rows = send_ref.shape[2]
    chunks = spheres // LANES
    for r in range(rows):
        cols = slice(r * LANES, (r + 1) * LANES)
        ends_s[pl.ds(r, 3, stride=padded), :] = ends_ref[:, cols]
        geo_s[pl.ds(r, 5, stride=padded), :] = geo_ref[:, cols]
    for r in range(chunks):
        dense_ref[pl.ds(r, FIELDS, stride=chunks), :] = force_ref[:, r * LANES : (r + 1) * LANES]
    first = ends_s[0:padded, :]
    second = ends_s[padded : 2 * padded, :]
    slot = ends_s[2 * padded : 3 * padded, :]
    inside = iota((padded, LANES), 0) < rows
    live = jnp.logical_and(slot < K, inside)
    shift = log2(spheres)
    first_block = first >> shift
    second_block = second >> shift
    owner = first_block >> log2(strips)
    apart = (second_block >> log2(strips)) ^ owner
    slab = jnp.where(apart == 0, 1, jnp.where(apart == 1, 2, 0))
    apart = (second_block ^ first_block) & (strips - 1)
    strip = jnp.where(apart == 0, 0, jnp.where(apart == 1, 1, 2))
    column = (strip * 3 + slab) * spheres + (second & (spheres - 1))
    place = first & (spheres - 1)
    tile = slot * (spheres // TILE) + (place >> log2(TILE))
    target = ((place & (LANES - 1)) * SUB + ((place >> log2(LANES)) & (SUB - 1))) * (K * spheres // TILE) + tile
    owner = jnp.where(live, owner, slabs)
    sep = [geo_s[c * padded : (c + 1) * padded, :] for c in range(3)]
    a = geo_s[3 * padded : 4 * padded, :]
    b = geo_s[4 * padded : 5 * padded, :]
    h = a + b
    total = sep[0] * sep[0] + sep[1] * sep[1] + sep[2] * sep[2] + h * h
    inv = lax.rsqrt(total)
    values = [target.astype(f32), column.astype(f32)] + [d * inv for d in sep] + [a * b * h * (inv * inv)]
    for c, value in enumerate(values):
        out_s[c, 0:padded, :] = value
    lane = iota((cap_rows, LANES), 1)
    place = iota((cap_rows, LANES), 0) * LANES + lane
    ends = [jnp.sum(jnp.where(owner <= o, 1.0, 0.0)).astype(i32) for o in range(slabs)]
    start = jnp.int32(0)
    for o in range(slabs):
        end = ends[o]
        row = start >> 7
        off = start & (LANES - 1)
        back = (LANES - off) & (LANES - 1)
        for c in range(SENT):
            rolled = pltpu.roll(out_s[c, pl.ds(row, cap_rows + SUB), :], back, 1)
            value = jnp.where(lane < LANES - off, rolled[:cap_rows], rolled[1 : cap_rows + 1])
            if c == 0:
                value = jnp.where(place < end - start, value, -1.0)
            send_ref[o, c] = value
        start = end


def pack(ends, geo, forces, slabs, strips):
    spheres = forces.shape[1]
    cap_rows = spheres * K // slabs // LANES
    rows = ends.shape[1] // LANES
    padded = -(-rows // SUB) * SUB
    return pl.pallas_call(
        functools.partial(pack_kernel, slabs, strips, spheres),
        out_shape=(
            jax.ShapeDtypeStruct((slabs, SENT, cap_rows, LANES), f32),
            jax.ShapeDtypeStruct((FIELDS * spheres // LANES, LANES), f32),
        ),
        scratch_shapes=[
            pltpu.VMEM((3 * padded, LANES), i32),
            pltpu.VMEM((5 * padded, LANES), f32),
            pltpu.VMEM((SENT, padded + cap_rows + SUB, LANES), f32),
        ],
        name="pack",
    )(ends, geo, forces)


def place_ranges(got_ref, tab_v):
    sources, _, cap_rows, _ = got_ref.shape
    tiles = sources * cap_rows // SUB
    lane = iota((SUB, LANES), 1)
    lane_f = lane.astype(f32)
    big = float(1 << 20)
    for group in range(sources // SUB):
        low = jnp.full((SUB, LANES), big, f32)
        high = jnp.full((SUB, LANES), -1.0, f32)
        for k in range(cap_rows):
            t = got_ref[group * SUB : (group + 1) * SUB, 0, k, :]
            tile = t - float(tiles) * jnp.floor(t * (1.0 / tiles))
            t_low = jnp.min(jnp.where(t < 0.0, big, tile), axis=1, keepdims=True)
            t_high = jnp.max(jnp.where(t < 0.0, -1.0, tile), axis=1, keepdims=True)
            low = jnp.where(lane == k, t_low, low)
            high = jnp.where(lane == k, t_high, high)
        starts = jnp.zeros((SUB, LANES), f32)
        counts = jnp.zeros((SUB, LANES), f32)
        for q in range(tiles):
            hit = jnp.logical_and(low <= q, high >= q)
            k_low = jnp.min(jnp.where(hit, lane_f, float(cap_rows - 1)), axis=1, keepdims=True)
            k_high = jnp.max(jnp.where(hit, lane_f, -1.0), axis=1, keepdims=True)
            starts = jnp.where(lane == q, k_low, starts)
            counts = jnp.where(lane == q, k_high - k_low + 1.0, counts)
        tab_v[group, 0] = starts.astype(i32)
        tab_v[group, 1] = jnp.broadcast_to(jnp.max(counts, axis=0, keepdims=True), (SUB, LANES)).astype(i32)


def place_sort(got_ref, pos_ref):
    sources, _, cap_rows, _ = got_ref.shape
    tiles = sources * cap_rows // SUB
    dims = (tiles, SUB, LANES)
    tile_bits, sub_bits = log2(tiles), log2(SUB)
    bits = log2(tiles * TILE)
    empty = 1 << (2 * bits)
    t = got_ref[:, 0].reshape(dims).astype(i32)
    home = (iota(dims, 0) * SUB + iota(dims, 1)) * LANES + iota(dims, 2)
    x = jnp.where(t < 0, empty, t << bits) + home
    place = (iota(dims, 2) * SUB + iota(dims, 1)) * tiles + iota(dims, 0)

    def partner(x, bit):
        axis, size, d = (1, SUB, 1 << (bit - tile_bits)) if bit < tile_bits + sub_bits else (
            2, LANES, 1 << (bit - tile_bits - sub_bits))
        if 2 * d == size:
            return pltpu.roll(x, d, axis)
        if axis == 1:
            at = iota((SUB, LANES), 0) ^ d
            return jnp.stack([jnp.take_along_axis(x[n], at, axis=0) for n in range(tiles)])
        upper = (iota(dims, axis) & d) != 0
        return jnp.where(upper, pltpu.roll(x, d, axis), pltpu.roll(x, size - d, axis))

    def exchange(x, bit):
        if bit < tile_bits:
            pairs = x.reshape((tiles >> (bit + 1), 2, 1 << bit, SUB, LANES))
            low = jnp.minimum(pairs[:, 0:1], pairs[:, 1:2])
            high = jnp.maximum(pairs[:, 0:1], pairs[:, 1:2])
            return jnp.concatenate([low, high], axis=1).reshape(dims)
        other = partner(x, bit)
        upper = (place & (1 << bit)) != 0
        return jnp.where(jnp.logical_xor(x < other, upper), x, other)

    for m in range(1, bits + 1):
        flip = -(((place >> m) ^ (place >> (m - 1) if m > 1 else 0)) & 1)
        x = x ^ flip
        for bit in range(m - 1, -1, -1):
            x = exchange(x, bit)

    def carry(x):
        x = pltpu.roll(x, 1, 1)
        return jnp.where(iota(x.shape, 1) < 1, pltpu.roll(x, 1, 2), x)

    for bit in range(bits - 1, -1, -1):
        move = jnp.logical_and(x < empty, x - (place << bits) >= (1 << (bit + bits)))
        y = jnp.where(move, x, empty)
        x = jnp.where(move, empty, x)
        if bit < tile_bits:
            d = 1 << bit
            y = jnp.concatenate([carry(y[tiles - d :]), y[: tiles - d]], axis=0)
        elif bit < tile_bits + sub_bits:
            d = 1 << (bit - tile_bits)
            y = pltpu.roll(y, d, 1)
            y = jnp.where(iota(dims, 1) < d, pltpu.roll(y, 1, 2), y)
        else:
            y = pltpu.roll(y, 1 << (bit - tile_bits - sub_bits), 2)
        x = jnp.minimum(x, y)
    pos_ref[...] = jnp.where(x < empty, x & ((1 << bits) - 1), -1)


def place_pick(spheres, got_ref, tab_s, pos_ref, terms_ref, col_ref):
    sources, _, cap_rows, _ = got_ref.shape
    groups = range(sources // SUB)
    tiles = K * spheres // TILE

    def pick(q, pos, group, kk, values):
        number = pos >> log2(LANES)
        at = pos & (LANES - 1)
        values = list(values)
        for u in range(SUB):
            s = group * SUB + u
            k = jnp.minimum(tab_s[group, 0, u, q] + kk, cap_rows - 1)
            match = number == s * cap_rows + k
            for c in range(1, SENT):
                row = jnp.broadcast_to(got_ref[s, c, pl.ds(k, 1), :], (SUB, LANES))
                found = jnp.take_along_axis(row, at, axis=1)
                values[c - 1] = jnp.where(match, found, values[c - 1])
        return tuple(values)

    def save(q, values):
        rows = pl.ds(pl.multiple_of(q * SUB, SUB), SUB)
        col_ref[rows, :] = values[0].astype(i32)
        for c in range(SENT - 2):
            terms_ref[c, rows, :] = values[c + 1]

    def first_rows(q, carry):
        pos = pos_ref[q]
        zero = jnp.zeros((SUB, LANES), f32)
        values = (jnp.where(pos >= 0, 0.0, -1.0),) + (zero,) * (SENT - 2)
        for group in groups:
            values = pick(q, pos, group, 0, values)
        save(q, values)
        return carry

    def more_rows(q, carry):
        for group in groups:
            count = tab_s[group, 1, 0, q]

            @pl.when(count > 1)
            def _():
                rows = pl.ds(pl.multiple_of(q * SUB, SUB), SUB)
                pos = pos_ref[q]
                values = (col_ref[rows, :].astype(f32),) + tuple(terms_ref[c, rows, :] for c in range(SENT - 2))
                values = lax.fori_loop(1, count, lambda kk, values: pick(q, pos, group, kk, values), values)
                save(q, values)

        return carry

    lax.fori_loop(0, tiles, first_rows, 0, unroll=8)
    lax.fori_loop(0, tiles, more_rows, 0)


def place_blocks(spheres, col_ref, span_ref):
    lane = iota((SUB, LANES), 1)
    big = float(1 << 20)
    low = jnp.full((SUB, LANES), big, f32)
    high = jnp.full((SUB, LANES), -1.0, f32)
    for q in range(K * spheres // (SUB * LANES)):
        block = (col_ref[q * SUB : (q + 1) * SUB, :] >> log2(spheres)).astype(f32)
        b_low = jnp.min(jnp.where(block < 0.0, big, block), axis=1, keepdims=True)
        b_high = jnp.max(block, axis=1, keepdims=True)
        low = jnp.where(lane == q, b_low, low)
        high = jnp.where(lane == q, b_high, high)
    span_ref[0:SUB, :] = jnp.broadcast_to(jnp.min(low, axis=0, keepdims=True), (SUB, LANES)).astype(i32)
    span_ref[SUB : 2 * SUB, :] = jnp.broadcast_to(jnp.max(high, axis=0, keepdims=True), (SUB, LANES)).astype(i32)


def tile_terms(terms_ref, rows, diff):
    e = [terms_ref[c, rows, :] for c in range(3)]
    c1 = terms_ref[3, rows, :]
    size = e[0] * e[0] + e[1] * e[1] + e[2] * e[2]
    c2 = c1 * (1.0 - size)
    p = e[0] * diff[0] + e[1] * diff[1] + e[2] * diff[2]
    t = e[0] * diff[3] + e[1] * diff[4] + e[2] * diff[5]
    mix = 0.8 * c1
    along_top = 6.0 * c2 * p + mix * t
    along_bottom = mix * p - 2.0 * c1 * t
    cross = mix * (size * (1.0 / 3.0))
    strong = 2.5 * c1
    top = [e[c] * along_top + c1 * diff[c] - cross * diff[3 + c] for c in range(3)]
    return top + [e[c] * along_bottom - cross * diff[c] + strong * diff[3 + c] for c in range(3)]


class Slot:
    def __init__(self, k, halves, span_ref, col_ref):
        self.halves = halves
        self.rows = [pl.ds(pl.multiple_of((k * halves + h) * SUB, SUB), SUB) for h in range(halves)]
        col = [col_ref[r, :] for r in self.rows]
        self.at = [c & (LANES - 1) for c in col]
        self.number = [c >> log2(LANES) for c in col]
        self.low = span_ref[0, k * halves]
        self.high = span_ref[SUB, k * halves]
        for h in range(1, halves):
            self.low = jnp.minimum(self.low, span_ref[0, k * halves + h])
            self.high = jnp.maximum(self.high, span_ref[SUB, k * halves + h])

    def none(self):
        return tuple(jnp.zeros((SUB, LANES), f32) for _ in range(FIELDS * self.halves))

    def gather(self, strip, part, values):
        chunks = part.shape[2]

        def block(b, values):
            values = list(values)
            for r in range(chunks):
                match = [n == b * chunks + r for n in self.number]
                for c in range(FIELDS):
                    row = jnp.broadcast_to(part[b - 3 * strip, c, r : r + 1, :], (SUB, LANES))
                    for h in range(self.halves):
                        found = jnp.take_along_axis(row, self.at[h], axis=1)
                        values[h * FIELDS + c] = jnp.where(match[h], found, values[h * FIELDS + c])
            return tuple(values)

        start = jnp.maximum(self.low, 3 * strip)
        return lax.fori_loop(start, jnp.minimum(self.high, 3 * strip + 2) + 1, block, values)


def apply_inner(mid, near, span_ref, col_ref, terms_ref, drag_ref, out_ref):
    chunks = mid.shape[2]
    halves = chunks // SUB

    def own(h, c):
        return mid[1, c, h * SUB : (h + 1) * SUB, :]

    def slot(k, sums):
        here = Slot(k, halves, span_ref, col_ref)
        other = here.gather(1, near, here.gather(0, mid, here.none()))
        sums = list(sums)
        for h in range(halves):
            diff = [own(h, c) - other[h * FIELDS + c] for c in range(FIELDS)]
            for c, term in enumerate(tile_terms(terms_ref, here.rows[h], diff)):
                sums[h * FIELDS + c] = sums[h * FIELDS + c] + term
        return tuple(sums)

    start = []
    for h in range(halves):
        for c in range(FIELDS):
            start.append(drag_ref[c * chunks + h * SUB : c * chunks + (h + 1) * SUB, :] * own(h, c))
    sums = lax.fori_loop(0, K, slot, tuple(start))
    for h in range(halves):
        for c in range(FIELDS):
            out_ref[c, h * SUB : (h + 1) * SUB, :] = sums[h * FIELDS + c]


def apply_outer(far, span_ref, col_ref, terms_ref, part_ref, out_ref):
    halves = far.shape[2] // SUB
    out_ref[...] = part_ref[...]

    def slot(k, carry):
        here = Slot(k, halves, span_ref, col_ref)

        @pl.when(here.high >= 6)
        def _():
            other = here.gather(2, far, here.none())
            for h in range(halves):
                terms = tile_terms(terms_ref, here.rows[h], other[h * FIELDS : (h + 1) * FIELDS])
                for c, term in enumerate(terms):
                    rows = slice(h * SUB, (h + 1) * SUB)
                    out_ref[c, rows, :] = out_ref[c, rows, :] - term

        return carry

    lax.fori_loop(0, K, slot, 0)


def two_sum(a, b):
    s = a + b
    t = s - a
    return s, (a - (s - t)) + (b - t)


def quick(a, b):
    s = a + b
    return s, b - (s - a)


def halve(a):
    t = a * 4097.0
    high = t - (t - a)
    return high, a - high


def two_prod(a, b, a_parts=None, b_parts=None):
    ah, al = a_parts or halve(a)
    bh, bl = b_parts or halve(b)
    p = a * b
    return p, ((ah * bh - p) + ah * bl + al * bh) + al * bl


class Pair:
    def __init__(self, high, low):
        self.high, self.low = high, low

    def __add__(self, other):
        s, e = two_sum(self.high, other.high)
        return Pair(*quick(s, e + (self.low + other.low)))

    def __neg__(self):
        return Pair(-self.high, -self.low)

    def __mul__(self, other):
        p, e = two_prod(self.high, other.high)
        return Pair(*quick(p, e + (self.high * other.low + self.low * other.high)))

    def __truediv__(self, other):
        q = self.high / other.high
        p, e = two_prod(q, other.high)
        rest = ((self.high - p) - e) + (self.low - q * other.low)
        return Pair(*quick(q, rest / other.high))


GRAM = [(a, b) for a in range(ITERS + 1) for b in range(a, ITERS + 1)]
EARLY = [n for n, (a, b) in enumerate(GRAM) if b < ITERS]
LATE = [n for n, (a, b) in enumerate(GRAM) if b == ITERS]


def gram_row(vectors, wanted):
    zero = jnp.zeros((SUB, LANES), f32)
    sums = [(zero, zero) for _ in wanted]
    fields, chunks, _ = vectors[0].shape
    for c in range(fields):
        for h in range(chunks // SUB):
            x = [v[c, h * SUB : (h + 1) * SUB, :] for v in vectors]
            parts = [halve(a) for a in x]
            for n, (a, b) in enumerate(GRAM[w] for w in wanted):
                p, e = two_prod(x[a], x[b], parts[a], parts[b])
                s, rest = two_sum(sums[n][0], p)
                sums[n] = (s, sums[n][1] + (e + rest))
    lane = iota((SUB, LANES), 1)
    sub = iota((SUB, LANES), 0)
    row = zero
    for base in range(0, len(wanted), SUB):
        packed = (zero, zero)
        spot = zero.astype(i32) - 1
        for n in range(base, min(base + SUB, len(wanted))):
            spot = jnp.where(sub == n - base, wanted[n], spot)
            s, e = sums[n]
            for step in (4, 2, 1):
                s, rest = two_sum(s, pltpu.roll(s, step, 0))
                e = e + pltpu.roll(e, step, 0) + rest
            packed = tuple(jnp.where(sub == n - base, new, old) for new, old in zip((s, e), packed))
        s, e = packed
        for step in (64, 32, 16, 8, 4, 2, 1):
            s, rest = two_sum(s, pltpu.roll(s, step, 1))
            e = e + pltpu.roll(e, step, 1) + rest
        row = row + jnp.where(lane == spot, s, 0.0)
        row = row + jnp.where(jnp.logical_and(spot >= 0, lane == spot + 64), e, 0.0)
    return jnp.sum(row, axis=0, keepdims=True)


def gram_total(rows_ref):
    total = Pair(jnp.zeros((SUB, LANES), f32), jnp.zeros((SUB, LANES), f32))
    for n in range(rows_ref.shape[0] // SUB):
        x = rows_ref[n * SUB : (n + 1) * SUB, :]
        total = total + Pair(x, pltpu.roll(x, 64, 1))
    for step in (4, 2, 1):
        total = total + Pair(pltpu.roll(total.high, step, 0), pltpu.roll(total.low, step, 0))
    grid = {}
    for n, (a, b) in enumerate(GRAM):
        at = jnp.full((SUB, LANES), n, i32)
        grid[a, b] = grid[b, a] = Pair(*quick(*(jnp.take_along_axis(x, at, axis=1) for x in (total.high, total.low))))
    return grid


def weigh(grid, x, y, shift):
    out = None
    for i, a in enumerate(x):
        for j, b in enumerate(y):
            term = grid[i, j + shift] if a is None and b is None else None
            if term is None:
                term = grid[i, j + shift] * (a if b is None else b if a is None else a * b)
            out = term if out is None else out + term
    return out


def conjugate(grid):
    zero = jnp.zeros((SUB, LANES), f32)
    one = Pair(zero + 1.0, zero)
    c = [one]
    d = [one]
    x = []
    norm = grid[0, 0]
    least = None
    for iteration in range(ITERS):
        step = norm / weigh(grid, d, d, 1)
        x = [a + step * b if a is not None else step * b for a, b in zip(x + [None], d)]
        c = [
            (c[n] if n < len(c) else None, -(step * d[n - 1]) if n else None) for n in range(len(d) + 1)
        ]
        c = [a if b is None else b if a is None else a + b for a, b in c]
        new = weigh(grid, c, c, 0)
        least = new.high if least is None else jnp.minimum(least, new.high)
        ratio = new / norm
        d = [a + ratio * b if b is not None else a for a, b in zip(c, d + [None])]
        norm = new
    size = zero
    for n in range(ITERS + 1):
        size = size + jnp.abs(c[n].high) * jnp.sqrt(grid[n, n].high)
    return [a.high for a in x], [a.high for a in c], jnp.where(least > 1e-6 * (size * size), 1.0, 0.0)


def first_kernel(
    spheres, got, drag, mid, near, terms, col, span, drag_out, part, pos, tab, tab_s, span_s, sem
):
    chunks = spheres // LANES
    place_ranges(got, tab)
    copy = pltpu.make_async_copy(tab, tab_s, sem)
    copy.start()
    for r in range(chunks):
        drag_out[pl.ds(r, FIELDS, stride=chunks), :] = drag[:, r * LANES : (r + 1) * LANES]
    place_sort(got, pos)
    copy.wait()
    place_pick(spheres, got, tab_s, pos, terms, col)
    place_blocks(spheres, col, span)
    copy = pltpu.make_async_copy(span, span_s, sem)
    copy.start()
    copy.wait()
    apply_inner(mid, near, span_s, col, terms, drag_out, part)


def inner_kernel(span, col, terms, drag, mid, near, part):
    apply_inner(mid, near, span, col, terms, drag, part)


def outer_kernel(span, col, terms, part, far, out):
    apply_outer(far, span, col, terms, part, out)


def inner_gram_kernel(span, col, terms, drag, mid, near, k0, k1, part, row):
    apply_inner(mid, near, span, col, terms, drag, part)
    row[...] = jnp.broadcast_to(gram_row([k0, k1, mid.at[1]], EARLY), row.shape)


def outer_gram_kernel(span, col, terms, part, far, k0, k1, k2, row, out, rows):
    apply_outer(far, span, col, terms, part, out)
    late = row[0:1, :] + gram_row([k0, k1, k2, out], LATE)
    rows[...] = jnp.broadcast_to(late, rows.shape)


def last_kernel(rows, k0, k1, k2, k3, velocity, residual, good, dense, flat, sem):
    x, c, ok = conjugate(gram_total(rows))
    chunks = k0.shape[1]
    k = [k0, k1, k2, k3]
    for n in range(k0.shape[0]):
        for h in range(chunks // SUB):
            part = [a[n, h * SUB : (h + 1) * SUB, :] for a in k]
            here = slice(n * chunks + h * SUB, n * chunks + (h + 1) * SUB)
            dense[0, here, :] = x[0] * part[0] + x[1] * part[1] + x[2] * part[2]
            dense[1, here, :] = part[0] + c[1] * part[1] + c[2] * part[2] + c[3] * part[3]
    copies = []
    for out, target in enumerate((velocity, residual)):
        for r in range(chunks):
            flat[out, :, r * LANES : (r + 1) * LANES] = dense[out, pl.ds(r, FIELDS, stride=chunks), :]
        copies.append(pltpu.make_async_copy(flat.at[out], target, sem.at[out]))
        copies[-1].start()
    good[0, 0] = jnp.min(ok).astype(i32)
    for copy in copies:
        copy.wait()


VMEM = pl.BlockSpec(memory_space=pltpu.VMEM)
SMEM = pl.BlockSpec(memory_space=pltpu.SMEM)
HBM = pl.BlockSpec(memory_space=pltpu.HBM)
PARAMS = pltpu.CompilerParams(vmem_limit_bytes=24 << 20)


def shape(dims, dtype=f32):
    return jax.ShapeDtypeStruct(dims, dtype)


def ring(axis, step):
    count = lax.axis_size(axis)
    return [(i, (i + step) % count) for i in range(count)]


def partners(axis):
    count = lax.axis_size(axis)
    return [(i, i ^ 1) for i in range(count)], [(i, (i + 1 if i % 2 else i - 1) % count) for i in range(count)]


def beside(x):
    pairs, others = partners("gx")
    far = lax.ppermute(x, "gx", others)
    near = lax.ppermute(x, "gx", pairs)
    mid = jnp.stack([far, x, near])
    pairs, others = partners("gy")
    return mid, lax.ppermute(mid, "gy", pairs), lax.ppermute(mid, "gy", others)


def plain(apply, forces):
    def both(a, b):
        return lax.psum(jnp.sum(a * b), ("gx", "gy"))

    velocity = jnp.zeros_like(forces)
    residual = direction = forces
    norm = both(residual, residual)
    for iteration in range(ITERS):
        applied = apply(direction)
        step = norm / both(direction, applied)
        velocity = velocity + step * direction
        residual = residual - step * applied
        new = both(residual, residual)
        direction = residual + new / norm * direction
        norm = new
    return velocity, residual


def on_device(pair_ends, pair_geometry, drag_coef, forces):
    spheres = drag_coef.shape[1]
    chunks = spheres // LANES
    slabs = lax.axis_size("gx")
    devices = slabs * lax.axis_size("gy")
    field = (FIELDS, chunks, LANES)
    slot_rows = K * spheres // LANES
    ranges = (slabs // SUB, 2, SUB, LANES)
    assert K * spheres == SUB * 4 * TILE and slabs % SUB == 0
    send, k0 = pack(pair_ends, pair_geometry, forces, slabs, lax.axis_size("gy"))
    got = lax.all_to_all(send, "gx", split_axis=0, concat_axis=0, tiled=True)
    k0 = k0.reshape(field)
    mid, near, far = beside(k0)
    terms, col, span, drag, part = pl.pallas_call(
        functools.partial(first_kernel, spheres),
        out_shape=(
            shape((SENT - 2, slot_rows, LANES)),
            shape((slot_rows, LANES), i32),
            shape((2 * SUB, LANES), i32),
            shape((FIELDS * chunks, LANES)),
            shape(field),
        ),
        in_specs=[VMEM] * 4,
        scratch_shapes=[
            pltpu.VMEM((slot_rows // SUB, SUB, LANES), i32),
            pltpu.VMEM(ranges, i32),
            pltpu.SMEM(ranges, i32),
            pltpu.SMEM((2 * SUB, LANES), i32),
            pltpu.SemaphoreType.DMA,
        ],
        compiler_params=PARAMS,
        cost_estimate=pl.CostEstimate(flops=0, bytes_accessed=48 << 20, transcendentals=0),
        name="first",
    )(got, drag_coef, mid, near)

    def local(kernel, name, outs, cost, *args):
        return pl.pallas_call(
            kernel,
            out_shape=outs,
            in_specs=[SMEM] + [VMEM] * (len(args) + 2),
            compiler_params=PARAMS,
            cost_estimate=pl.CostEstimate(flops=0, bytes_accessed=cost << 20, transcendentals=0),
            name=name,
        )(span, col, terms, *args)

    k1 = local(outer_kernel, "outer", shape(field), 16, part, far)

    def apply(x):
        mid, near, far = beside(x)
        part = local(inner_kernel, "inner", shape(field), 16, drag, mid, near)
        return local(outer_kernel, "outer", shape(field), 16, part, far)

    k2 = apply(k1)
    mid, near, far = beside(k2)
    part, row = local(
        inner_gram_kernel, "inner_gram", (shape(field), shape((SUB, LANES))), 16, drag, mid, near, k0, k1
    )
    k3, rows = local(
        outer_gram_kernel, "outer_gram", (shape(field), shape((devices, LANES))), 16, part, far, k0, k1, k2, row
    )
    rows = lax.all_to_all(rows, ("gx", "gy"), split_axis=0, concat_axis=0, tiled=True)
    velocity, residual, good = pl.pallas_call(
        last_kernel,
        out_shape=(shape((FIELDS, spheres)), shape((FIELDS, spheres)), shape((1, 1), i32)),
        out_specs=(HBM, HBM, SMEM),
        scratch_shapes=[
            pltpu.VMEM((2, FIELDS * chunks, LANES), f32),
            pltpu.VMEM((2, FIELDS, spheres), f32),
            pltpu.SemaphoreType.DMA((2,)),
        ],
        compiler_params=PARAMS,
        name="last",
    )(rows, k0, k1, k2, k3)

    def again(state):
        v, r = plain(apply, k0)
        return jnp.ones_like(good), v.reshape(FIELDS, spheres), r.reshape(FIELDS, spheres)

    return lax.while_loop(lambda state: state[0][0, 0] == 0, again, (good, velocity, residual))[1:]


def solution(mesh):
    spec = P(None, ("gx", "gy"))
    return jax.shard_map(
        on_device, mesh=mesh, in_specs=(spec,) * 4, out_specs=(spec, spec), check_vma=False
    )
```
